512 devices in a mesh: section: 32 (over y, x, core), inner: 16 (over z).
Axes of the slice: x: 4, y: 4, z: 16, core: 2. Of those that a mesh axis runs over, the one named last changes fastest.
Arguments:
- tokens: bfloat16 [2, 512, 3072], P(None, 'section'), may hold values from -6 to 6
- norm_gain: float32 [3072], replicated, may hold values from 0.5 to 1.5
- router: bfloat16 [3072, 8], replicated, may hold values from -0.21875 to 0.21875
- expert_in: bfloat16 [32, 2, 4096, 3072], P('section', None, 'inner'), may hold values from -0.109375 to 0.109375
- expert_out: bfloat16 [32, 4096, 3072], P('section', 'inner'), may hold values from -0.09375 to 0.09375
- choices: int32 [2, 512, 2], P(None, 'section'), may hold values from 0 to 7, all different within a row; in each aligned block of 16 rows (0 to 15, 16 to 31, ..., all dimensions but the last counted through in order) at most 8 rows name the same one
Outputs:
- layer_outputs: bfloat16 [2, 512, 3072], P(None, 'section', 'inner')
The draws below stay inside these ranges and needn't reach their ends.
Inputs may be any that keep to these rules, and one draw needn't show every extreme that they name: `choices`: the two experts of a row differ; in each micro-batch the 16 rows of one section name any expert at most 8 times.
All inputs are finite; a program needn't handle non-finite values.
Results may differ from the reference program's by a relative error of at most 0.019.
Values may be sent and summed in bfloat16 or wider, within the bound.
A program may use at most 128 MiB of HBM per device.

```python
import math
import jax
import jax.numpy as jnp
import numpy as np
from jax import lax

D = 3072
E = 8
HID_DEV = 256
R_SEC = 16
MICRO = 2
CAP = 8
SPE = 4
HID_SEC = 4096
FF_WIN = 16384
ROWS = 512
N_INNER = 16


def block_levels(key, shape, cuts, least, high):
    level = 1.0
    for dim, parts in cuts:
        draws = jax.random.uniform(jax.random.fold_in(jax.random.fold_in(key, 6), dim), (parts,), jnp.float32, least / len(cuts), high / len(cuts))
        level = level * jnp.repeat(jnp.exp(draws), shape[dim] // parts).reshape((-1,) + (1,) * (len(shape) - 1 - dim))
    return level


def assign_block(key, own, number, rows, amount, top, reach, lean):
    order = jax.random.permutation(key, amount)
    packed, ordinary = portions_of(amount, rows * top, reach, lean, True), portions_of(amount, rows * top, reach, lean, False)
    places = jnp.arange(amount)

    def named(lengths, turn):
        used = int((lengths > 0).sum())
        fixed = max(1, used // 4)
        moved = fixed + (places - fixed + turn * (used - fixed)) % max(1, amount - fixed)
        return jnp.zeros((amount,), jnp.int32).at[order[jnp.where(places < fixed, places, moved)]].set(jnp.asarray(lengths, jnp.int32))

    lengths = jnp.where(number % 4 == 0, named(packed, number // 4), named(ordinary, number - number // 4 - 1))
    mixed = jax.random.permutation(jax.random.fold_in(own, 3), amount)
    giver, sink = mixed[0:amount // 2 * 2:2], mixed[1:amount // 2 * 2:2]
    margin = jnp.minimum(lengths[giver] - 1, reach - lengths[sink]) // 2
    margin = jnp.where((giver == order[0]) | (sink == order[0]) | (lengths[sink] == 0), 0, jnp.maximum(margin, 0))
    moved = jax.random.randint(jax.random.fold_in(own, 4), (amount // 2,), 0, 1 << 20) % (margin + 1)
    lengths = lengths.at[giver].add(-moved).at[sink].add(moved)
    items = jnp.searchsorted(jnp.cumsum(lengths), jnp.arange(rows * top), side="right").astype(jnp.int32)
    listing = items.reshape(top, rows).T
    listing = listing[jax.random.permutation(jax.random.fold_in(own, 1), rows)]
    turn = jax.random.randint(jax.random.fold_in(own, 2), (rows, 1), 0, top)
    return jnp.take_along_axis(listing, (jnp.arange(top)[None, :] + turn) % top, axis=1)


def portions_of(count, total, bound, lean, full):
    loads = [(1 << 20) // math.isqrt(standing ** lean) + 1 for standing in range(1, count + 1)]
    largest = bound if full else min(bound, max(-(-total // count), total * loads[0] // sum(loads)))
    least = 1 if total - largest >= count - 1 else 0
    counts, surplus = [largest] + [least] * (count - 1), total - largest - least * (count - 1)
    while surplus > 0:
        candidates = [i for i in range(1, count) if counts[i] < largest] or [i for i in range(1, count) if counts[i] < bound]
        mass, remaining = sum([loads[i] for i in candidates]), surplus
        for i in candidates:
            addition = min(bound - counts[i], max(1, remaining * loads[i] // mass), surplus)
            counts[i] = counts[i] + addition
            surplus = surplus - addition
    return np.array(counts)


def gaussian(stream_key, dims, scale, most, pieces=(), kind=jnp.bfloat16):
    array = jax.random.normal(stream_key, dims, jnp.float32) * scale
    if len(pieces) > 0:
        array = block_levels(stream_key, dims, pieces, -0.22, 0.18) * array
    return jnp.clip(array, min=-most, max=most).astype(kind)


def setup_inputs(seed: int = 0) -> dict:
    streams_of = jax.random.split(jax.random.key(seed), 7)
    tokens = gaussian(streams_of[0], (MICRO, ROWS, D), 1.0, 6.0, ((1, 32),))
    norm_gain = jnp.clip(jax.random.uniform(streams_of[1], (D,), jnp.float32, 0.5, 1.5), 0.5, 1.5)
    router = gaussian(streams_of[2], (D, E), (D // 4) ** -0.5, 0.21875)
    expert_in = gaussian(streams_of[3], (E * SPE, 2, HID_SEC, D), D ** -0.5, 0.109375, ((0, 32), (2, 16)))
    expert_out = gaussian(streams_of[4], (E * SPE, HID_SEC, D), (FF_WIN // 4) ** -0.5, 0.09375, ((0, 32), (1, 16)))
    choices_keys = jax.random.split(jax.random.fold_in(streams_of[5], 1), MICRO * ROWS // R_SEC)
    choices_turns = jax.random.permutation(jax.random.fold_in(streams_of[5], 3), MICRO * ROWS // R_SEC)
    choices = jax.vmap(lambda own, number: assign_block(jax.random.fold_in(streams_of[5], 2), own, number, R_SEC, E, 2, CAP, 2))(choices_keys, choices_turns).reshape((MICRO, ROWS, 2))
    return {"tokens": tokens, "norm_gain": norm_gain, "router": router, "expert_in": expert_in, "expert_out": expert_out, "choices": choices}


epsilon = 1e-05

def reference(tokens, norm_gain, router, expert_in, expert_out, choices):
    w_in_all = expert_in.reshape(E, SPE, 2, HID_SEC, D)
    w_out_all = expert_out.reshape(E, SPE * N_INNER, HID_DEV, D)
    expert_ids = jnp.arange(E, dtype=jnp.int32)
    results = []
    for micro_idx in range(MICRO):
        values = tokens[micro_idx].astype(jnp.float32)
        inv_rms = lax.rsqrt(lax.optimization_barrier(jnp.mean(values * values, axis=-1, keepdims=True)) + epsilon)
        normed = (values * inv_rms * norm_gain).astype(jnp.bfloat16)
        logits = jnp.dot(normed, router, preferred_element_type=jnp.float32)
        chosen = choices[micro_idx]
        first_hot = (chosen[:, 0:1] == expert_ids[None, :]).astype(jnp.float32)
        second_hot = (chosen[:, 1:2] == expert_ids[None, :]).astype(jnp.float32)
        lead_logit = lax.optimization_barrier(jnp.sum(logits * first_hot, axis=1, keepdims=True))
        trail_logit = lax.optimization_barrier(jnp.sum(logits * second_hot, axis=1, keepdims=True))
        weight_a = 1.0 / (1.0 + jnp.exp(trail_logit - lead_logit))
        weight_b = 1.0 / (1.0 + jnp.exp(lead_logit - trail_logit))
        mixing = weight_a * first_hot + weight_b * second_hot
        normed_wide = normed.astype(jnp.float32)

        def expert_step(total, expert):
            w_in_e = lax.dynamic_index_in_dim(w_in_all, expert, 0, keepdims=False)
            w_out_e = lax.dynamic_index_in_dim(w_out_all, expert, 0, keepdims=False)
            gate_up = jnp.einsum('rd,jkfd->rjkf', normed_wide, w_in_e.astype(jnp.float32))
            active = (jax.nn.silu(gate_up[:, :, 0]) * gate_up[:, :, 1]).astype(jnp.bfloat16)
            active = active.reshape(ROWS, SPE * N_INNER, HID_DEV)

            def block_step(accum, block):
                act_block = lax.dynamic_index_in_dim(active, block, 1, keepdims=False)
                w_block = lax.dynamic_index_in_dim(w_out_e, block, 0, keepdims=False)
                part_out = jnp.dot(act_block, w_block, preferred_element_type=jnp.float32).astype(jnp.bfloat16)
                return (accum + part_out.astype(jnp.float32), None)
            expert_rows, _ = lax.scan(block_step, jnp.zeros((ROWS, D), jnp.float32), jnp.arange(SPE * N_INNER, dtype=jnp.int32))
            weight = lax.dynamic_index_in_dim(mixing, expert, 1, keepdims=True)
            return (total + weight * expert_rows, None)
        total, _ = lax.scan(expert_step, jnp.zeros((ROWS, D), jnp.float32), expert_ids)
        results.append((values + total).astype(jnp.bfloat16))
    return jnp.stack(results)
```

```python
import functools
import math

import jax
import jax.numpy as jnp
from jax import lax
from jax.experimental import pallas as pl
from jax.experimental.pallas import tpu as pltpu
from jax.sharding import PartitionSpec as P

epsilon = 1e-05
MESH = pl.DeviceIdType.MESH
BF16 = jnp.bfloat16
F32 = jnp.float32


def nt_dot(a, b):
    return lax.dot_general(a, b, (((1,), (1,)), ((), ())), preferred_element_type=F32)


def moe_kernel(
    sections,
    inners,
    experts,
    micro,
    tokens,
    gain,
    router,
    choices,
    w_in,
    w_out,
    out,
    normed,
    outgoing,
    slots,
    w_in_v,
    w_out_v,
    gate_up,
    active,
    mix_hi,
    mix_lo,
    pair_send,
    pair_recv,
    own,
    deep_send,
    deep_recv,
    back_send,
    back_recv,
    part_send,
    part_recv,
    w_sem,
    out_sem,
    in_sem,
    deep_out_sem,
    deep_in_sem,
    share_out_sem,
    share_in_sem,
    pair_out_sem,
    pair_in_sem,
    fold_out_sem,
    fold_in_sem,
    back_out_sem,
    back_in_sem,
    part_out_sem,
    part_in_sem,
):
    chips = sections // 2
    side = math.isqrt(chips)
    per_expert = chips // experts
    rows_all, width = tokens.shape
    rows = rows_all // micro
    cap = rows // 2
    tile = micro * cap
    q_width = width // 4
    hidden = w_out.shape[0]
    half_rows = chips * tile
    group_rows = side * tile
    slice_width = width // inners
    per_quarter = inners // 4

    section = lax.axis_index("section")
    z = lax.axis_index("inner")
    chip, core = section // 2, lax.rem(section, 2)
    chip_y, chip_x = chip // side, lax.rem(chip, side)
    parity = lax.rem(z, 2)
    z_up = lax.rem(z + 1, inners)
    z_down = lax.rem(z + inners - 1, inners)
    partner = chip * 2 + 1 - core
    deep_to = (z_up, z_down)
    fold_to = (z_down, z_up)
    mine = pl.multiple_of(core * half_rows, half_rows)
    theirs = pl.multiple_of((1 - core) * half_rows, half_rows)
    keep = (2 * parity, 2 * parity + 1)
    pass_on = (2 * (1 - parity), 2 * (1 - parity) + 1)

    def local(src, dst, sem):
        return pltpu.make_async_copy(src, dst, sem)

    def remote(src, dst, send, recv, to_section, to_inner):
        return pltpu.make_async_remote_copy(
            src_ref=src, dst_ref=dst, send_sem=send, recv_sem=recv, device_id=(to_section, to_inner), device_id_type=MESH
        )

    def took(view, sem):
        local(view, view, sem).wait()

    for q in range(4):
        local(w_in.at[:, pl.ds(q * q_width, q_width)], w_in_v.at[q], w_sem.at[q]).start()
    for q in range(4):
        local(w_out.at[:, pl.ds(q * q_width, q_width)], w_out_v.at[q], w_sem.at[4 + q]).start()

    offsets = [(dy, dx) for dy in range(side) for dx in range(side) if (dy, dx) != (0, 0)]
    offsets.sort(key=lambda o: (min(o[0], side - o[0]) + min(o[1], side - o[1]), o))

    def chip_at(dy, dx):
        return lax.rem(chip_y + dy, side) * side + lax.rem(chip_x + dx, side)

    barrier = pltpu.get_barrier_semaphore()
    for dy, dx in offsets:
        pl.semaphore_signal(barrier, inc=1, device_id=(chip_at(dy, dx) * 2 + core, z), device_id_type=MESH)
    pl.semaphore_signal(barrier, inc=1, device_id=(partner, z), device_id_type=MESH)
    for k in range(1, inners):
        pl.semaphore_signal(barrier, inc=1, device_id=(section, lax.rem(z + k, inners)), device_id_type=MESH)

    values = tokens[...].astype(F32)
    inv_rms = lax.rsqrt(jnp.mean(values * values, axis=-1, keepdims=True) + epsilon)
    normed_value = (values * inv_rms * gain[...]).astype(BF16)
    for q in range(4):
        normed[q] = normed_value[:, q * q_width : (q + 1) * q_width]
    logits = jnp.dot(normed_value, router[...], preferred_element_type=F32)
    first, second = choices[:, 0:1], choices[:, 1:2]

    def hot(index, name):
        return jnp.where(index == name, 1.0, 0.0).astype(F32)

    ids = lax.broadcasted_iota(jnp.int32, (rows_all, experts), 1)
    lead = jnp.sum(logits * hot(first, ids), axis=1, keepdims=True)
    trail = jnp.sum(logits * hot(second, ids), axis=1, keepdims=True)
    weight_a = 1.0 / (1.0 + jnp.exp(trail - lead))
    weight_b = 1.0 / (1.0 + jnp.exp(lead - trail))
    row_of = lax.broadcasted_iota(jnp.int32, (rows_all, rows_all), 0)
    col_of = lax.broadcasted_iota(jnp.int32, (rows_all, rows_all), 1)
    before = jnp.where((row_of // rows == col_of // rows) & (col_of < row_of), 1.0, 0.0).astype(BF16)

    def placing(columns, copies):
        col = lax.broadcasted_iota(jnp.int32, (rows_all, columns), 1)
        row = lax.broadcasted_iota(jnp.int32, (rows_all, columns), 0)
        name = col // (tile * copies)
        first_hot, second_hot = hot(first, name), hot(second, name)
        both = first_hot + second_hot
        rank = jnp.dot(before, both.astype(BF16), preferred_element_type=F32)
        seat = (lax.rem(col, tile) // cap == row // rows) & (rank == lax.rem(col, cap).astype(F32))
        return jnp.where(seat, both, 0.0), jnp.where(seat, weight_a * first_hot + weight_b * second_hot, 0.0)

    placed, _ = placing(experts * tile, 1)
    _, mixing = placing(chips * tile, per_expert)
    mixing_high = mixing.astype(BF16)
    mix_hi[...] = mixing_high
    mix_lo[...] = (mixing - mixing_high.astype(F32)).astype(BF16)
    placed_t = jnp.transpose(placed).astype(BF16)
    for i in range(2):
        picked = jnp.dot(placed_t, normed[keep[i]], preferred_element_type=F32).astype(BF16)
        outgoing[i] = picked.reshape(experts, tile, q_width)
    home = pl.multiple_of(mine + chip * tile, tile)
    for i in range(2):
        slots[keep[i], pl.ds(home, tile), :] = outgoing[i, chip // per_expert]

    pl.semaphore_wait(barrier, len(offsets) + 1 + inners - 1)

    for dy, dx in offsets:
        to = chip_at(dy, dx)
        for i in range(2):
            remote(
                outgoing.at[i, to // per_expert],
                slots.at[keep[i], pl.ds(home, tile), :],
                out_sem.at[0],
                in_sem.at[i, chip_y],
                to * 2 + core,
                z,
            ).start()

    def group_at(j):
        return lax.rem(chip_y + j, side)

    def group_of(j):
        return pl.ds(pl.multiple_of(mine + group_at(j) * group_rows, group_rows), group_rows)

    for j in range(side):
        for i in range(2):
            arrived = group_rows if j else group_rows - tile
            took(slots.at[keep[i], pl.ds(0, arrived), :], in_sem.at[i, group_at(j)])
            view = slots.at[keep[i], group_of(j), :]
            remote(view, view, deep_out_sem.at[0], deep_in_sem.at[i, group_at(j)], section, deep_to[i]).start()
            remote(view, view, share_out_sem.at[0], share_in_sem.at[0, i], partner, z).start()

    def project(q):
        for half in range(2):
            block = pl.ds(half * half_rows, half_rows)
            gate_up[block, :] += nt_dot(slots[q, block, :], w_in_v[q])

    gate_up[...] = jnp.zeros_like(gate_up)
    for q in range(4):
        took(w_in_v.at[q], w_sem.at[q])
    for i in range(2):
        took(slots.at[keep[i], pl.ds(0, half_rows), :], share_in_sem.at[0, i])
        project(keep[i])
    for j in range(side):
        for i in range(2):
            took(slots.at[pass_on[i], pl.ds(0, group_rows), :], deep_in_sem.at[i, group_at(j)])
            view = slots.at[pass_on[i], group_of(j), :]
            remote(view, view, share_out_sem.at[0], share_in_sem.at[1, i], partner, z).start()
    for i in range(2):
        took(slots.at[pass_on[i], pl.ds(0, half_rows), :], share_in_sem.at[1, i])
        project(pass_on[i])

    gate = gate_up[:, :hidden]
    active[...] = (gate / (1.0 + jnp.exp(-gate)) * gate_up[:, hidden:]).astype(BF16)

    for q in range(4):
        took(w_out_v.at[q], w_sem.at[4 + q])
    order = pass_on + keep
    for n, q in enumerate(order):
        pair_send[n] = jnp.dot(active[pl.ds(theirs, half_rows), :], w_out_v[q], preferred_element_type=F32).astype(BF16)
        remote(pair_send.at[n], pair_recv.at[n], pair_out_sem.at[0], pair_in_sem.at[n], partner, z).start()
    for n, q in enumerate(order):
        own[n] = jnp.dot(active[pl.ds(mine, half_rows), :], w_out_v[q], preferred_element_type=F32).astype(BF16)

    for i in range(2):
        took(pair_recv.at[i], pair_in_sem.at[i])
        deep_send[i] = (own[i].astype(F32) + pair_recv[i].astype(F32)).astype(BF16)
        remote(deep_send.at[i], deep_recv.at[i], fold_out_sem.at[0], fold_in_sem.at[i], section, fold_to[i]).start()
    for i in range(2):
        took(pair_recv.at[2 + i], pair_in_sem.at[2 + i])
        took(deep_recv.at[i], fold_in_sem.at[i])
        total = own[2 + i].astype(F32) + pair_recv[2 + i].astype(F32) + deep_recv[i].astype(F32)
        back_send[i] = total.astype(BF16)
        here = pl.ds(pl.multiple_of(chip * tile, tile), tile)
        back_recv[i, here, :] = back_send[i, here, :]
        for dy, dx in offsets:
            to = chip_at(dy, dx)
            there = pl.ds(pl.multiple_of(to * tile, tile), tile)
            remote(
                back_send.at[i, there, :], back_recv.at[i, here, :], back_out_sem.at[0], back_in_sem.at[i], to * 2 + core, z
            ).start()

    for i in range(2):
        took(back_recv.at[i, pl.ds(0, half_rows - tile), :], back_in_sem.at[i])
        total = jnp.dot(mix_hi[...], back_recv[i], preferred_element_type=F32) + jnp.dot(
            mix_lo[...], back_recv[i], preferred_element_type=F32
        )
        for j in range(per_quarter):
            shifted = total if j == 0 else pltpu.roll(total, q_width - j * slice_width, 1)
            n = i * per_quarter + j
            part_send[n] = shifted[:, :slice_width].astype(BF16)
            to = parity * (inners // 2) + n

            @pl.when(to == z)
            def _():
                local(part_send.at[n], part_recv.at[z // 2], part_in_sem.at[0]).start()

            @pl.when(to != z)
            def _():
                remote(part_send.at[n], part_recv.at[z // 2], part_out_sem.at[0], part_in_sem.at[0], section, to).start()

    took(part_recv, part_in_sem.at[0])
    total = part_recv[0].astype(F32)
    for k in range(1, inners // 2):
        total += part_recv[k].astype(F32)
    out[...] = total

    took(back_send.at[:, pl.ds(0, half_rows - tile), :], out_sem.at[0])
    took(back_send, deep_out_sem.at[0])
    took(pair_send, share_out_sem.at[0])
    took(pair_send, pair_out_sem.at[0])
    took(deep_send, fold_out_sem.at[0])
    took(back_send.at[:, pl.ds(0, half_rows - tile), :], back_out_sem.at[0])
    inside = z // (inners // 2) == parity

    @pl.when(inside)
    def _():
        took(part_send.at[pl.ds(0, inners // 2 - 1)], part_out_sem.at[0])

    @pl.when(jnp.logical_not(inside))
    def _():
        took(part_send, part_out_sem.at[0])


def body(tokens, norm_gain, router, expert_in, expert_out, choices):
    sections = lax.axis_size("section")
    inners = lax.axis_size("inner")
    member = lax.axis_index("inner")
    micro, rows, width = tokens.shape
    experts = router.shape[1]
    hidden = expert_in.shape[2]
    chips = sections // 2
    side = math.isqrt(chips)
    slice_width = width // inners
    q_width = width // 4
    rows_all = micro * rows
    tile = micro * (rows // 2)
    half_rows = chips * tile
    flat = tokens.reshape(rows_all, width)
    vmem = pl.BlockSpec(memory_space=pltpu.VMEM)
    anywhere = pl.BlockSpec(memory_space=pl.ANY)
    dma = pltpu.SemaphoreType.DMA
    moe = pl.pallas_call(
        functools.partial(moe_kernel, sections, inners, experts, micro),
        out_shape=jax.ShapeDtypeStruct((rows_all, slice_width), F32),
        in_specs=[vmem, vmem, vmem, vmem, anywhere, anywhere],
        out_specs=vmem,
        scratch_shapes=[
            pltpu.VMEM((4, rows_all, q_width), BF16),
            pltpu.VMEM((2, experts, tile, q_width), BF16),
            pltpu.VMEM((4, 2 * half_rows, q_width), BF16),
            pltpu.VMEM((4, 2 * hidden, q_width), BF16),
            pltpu.VMEM((4, hidden, q_width), BF16),
            pltpu.VMEM((2 * half_rows, 2 * hidden), F32),
            pltpu.VMEM((2 * half_rows, hidden), BF16),
            pltpu.VMEM((rows_all, half_rows), BF16),
            pltpu.VMEM((rows_all, half_rows), BF16),
            pltpu.VMEM((4, half_rows, q_width), BF16),
            pltpu.VMEM((4, half_rows, q_width), BF16),
            pltpu.VMEM((4, half_rows, q_width), BF16),
            pltpu.VMEM((2, half_rows, q_width), BF16),
            pltpu.VMEM((2, half_rows, q_width), BF16),
            pltpu.VMEM((2, half_rows, q_width), BF16),
            pltpu.VMEM((2, half_rows, q_width), BF16),
            pltpu.VMEM((inners // 2, rows_all, slice_width), BF16),
            pltpu.VMEM((inners // 2, rows_all, slice_width), BF16),
            dma((8,)),
            dma((1,)),
            dma((2, side)),
            dma((1,)),
            dma((2, side)),
            dma((1,)),
            dma((2, 2)),
            dma((1,)),
            dma((4,)),
            dma((1,)),
            dma((2,)),
            dma((1,)),
            dma((2,)),
            dma((1,)),
            dma((1,)),
        ],
        compiler_params=pltpu.CompilerParams(
            collective_id=0, has_side_effects=True, vmem_limit_bytes=48 * 1024 * 1024
        ),
    )(
        flat,
        norm_gain.reshape(1, width),
        router,
        choices.reshape(rows_all, 2),
        expert_in.reshape(2 * hidden, width),
        expert_out.reshape(hidden, width),
    )
    residual = lax.dynamic_slice_in_dim(flat, member * slice_width, slice_width, 1).astype(F32)
    return (residual + moe).astype(BF16).reshape(micro, rows, slice_width)


def solution(mesh):
    return jax.shard_map(
        body,
        mesh=mesh,
        in_specs=(
            P(None, "section", None),
            P(),
            P(),
            P("section", None, "inner", None),
            P("section", "inner", None),
            P(None, "section", None),
        ),
        out_specs=P(None, "section", "inner"),
        check_vma=False,
    )
```

```python
import functools
import math

import jax
import jax.numpy as jnp
from jax import lax
from jax.experimental import pallas as pl
from jax.experimental.pallas import tpu as pltpu
from jax.sharding import PartitionSpec as P

epsilon = 1e-05
MESH = pl.DeviceIdType.MESH
BF16 = jnp.bfloat16
F32 = jnp.float32


def nt_dot(a, b):
    return lax.dot_general(a, b, (((1,), (1,)), ((), ())), preferred_element_type=F32)


def moe_kernel(
    sections,
    inners,
    experts,
    micro,
    tokens_hbm,
    gain_hbm,
    router_hbm,
    choices_hbm,
    w_in,
    w_out,
    out,
    tokens,
    gain,
    router,
    choices,
    normed,
    outgoing,
    slots,
    w_in_v,
    w_out_v,
    active,
    mix,
    partial,
    pair_recv,
    deep_send,
    deep_recv,
    back_send,
    back_recv,
    part_send,
    part_recv,
    residual,
    small_sem,
    w_sem,
    out_sem,
    in_sem,
    deep_out_sem,
    deep_in_sem,
    share_out_sem,
    share_in_sem,
    pair_out_sem,
    pair_in_sem,
    fold_out_sem,
    fold_in_sem,
    back_out_sem,
    back_in_sem,
    part_out_sem,
    part_in_sem,
):
    chips = sections // 2
    side = math.isqrt(chips)
    per_expert = chips // experts
    rows_all, width = tokens.shape
    rows = rows_all // micro
    cap = rows // 2
    tile = micro * cap
    q_width = width // 4
    hidden = w_out.shape[0]
    half_rows = chips * tile
    group_rows = side * tile
    slice_width = width // inners
    per_quarter = inners // 4

    section = lax.axis_index("section")
    z = lax.axis_index("inner")
    chip, core = section // 2, lax.rem(section, 2)
    chip_y, chip_x = chip // side, lax.rem(chip, side)
    parity = lax.rem(z, 2)
    z_up = lax.rem(z + 1, inners)
    z_down = lax.rem(z + inners - 1, inners)
    partner = chip * 2 + 1 - core
    deep_to = (z_up, z_down)
    fold_to = (z_down, z_up)
    keep = 2 * parity
    pass_on = 2 * (1 - parity)

    def local(src, dst, sem):
        return pltpu.make_async_copy(src, dst, sem)

    def remote(src, dst, send, recv, to_section, to_inner):
        return pltpu.make_async_remote_copy(
            src_ref=src, dst_ref=dst, send_sem=send, recv_sem=recv, device_id=(to_section, to_inner), device_id_type=MESH
        )

    def took(view, sem):
        local(view, view, sem).wait()

    small = ((tokens_hbm, tokens), (gain_hbm, gain), (router_hbm, router), (choices_hbm, choices))
    for n, (src, dst) in enumerate(small):
        local(src, dst, small_sem.at[n]).start()
    for q in range(4):
        local(w_in.at[:, pl.ds(q * q_width, q_width)], w_in_v.at[q], w_sem.at[q]).start()
    for q in range(4):
        local(w_out.at[:, pl.ds(q * q_width, q_width)], w_out_v.at[q], w_sem.at[4 + q]).start()

    steps = sorted(range(side), key=lambda j: (j % 2, j))
    offsets = [(-j % side, dx) for j in steps for dx in range(side) if (j, dx) != (0, 0)]

    def place_of(y):
        return lax.rem(y, 2) * (side // 2) + y // 2

    my_place = place_of(chip_y)

    def chip_at(dy, dx):
        return lax.rem(chip_y + dy, side) * side + lax.rem(chip_x + dx, side)

    barrier = pltpu.get_barrier_semaphore()
    for dy, dx in offsets:
        pl.semaphore_signal(barrier, inc=1, device_id=(chip_at(dy, dx) * 2 + core, z), device_id_type=MESH)
    pl.semaphore_signal(barrier, inc=1, device_id=(partner, z), device_id_type=MESH)
    for k in range(1, inners):
        pl.semaphore_signal(barrier, inc=1, device_id=(section, lax.rem(z + k, inners)), device_id_type=MESH)

    for n, (src, dst) in enumerate(small):
        local(src, dst, small_sem.at[n]).wait()
    values = tokens[...].astype(F32)
    inv_rms = lax.rsqrt(jnp.mean(values * values, axis=-1, keepdims=True) + epsilon)
    normed_value = (values * inv_rms * gain[...]).astype(BF16)
    for q in range(4):
        normed[q] = normed_value[:, q * q_width : (q + 1) * q_width]
    row_of = lax.broadcasted_iota(jnp.int32, (rows, rows_all), 0)
    col_of = lax.broadcasted_iota(jnp.int32, (rows, rows_all), 1)
    chosen = jnp.zeros((2, rows_all), F32)
    for m in range(micro):
        spread = jnp.where(col_of == row_of + m * rows, 1.0, 0.0).astype(BF16)
        chosen += jnp.dot(choices[m].astype(F32).astype(BF16), spread, preferred_element_type=F32)
    first, second = chosen[0:1].astype(jnp.int32), chosen[1:2].astype(jnp.int32)
    row_of = lax.broadcasted_iota(jnp.int32, (rows_all, rows_all), 0)
    col_of = lax.broadcasted_iota(jnp.int32, (rows_all, rows_all), 1)
    before = jnp.where((row_of // rows == col_of // rows) & (row_of < col_of), 1.0, 0.0).astype(BF16)

    def hot(index, name):
        return jnp.where(index == name, 1.0, 0.0).astype(F32)

    def seats(count, copies):
        seat_of = lax.broadcasted_iota(jnp.int32, (count, rows_all), 0)
        row_of = lax.broadcasted_iota(jnp.int32, (count, rows_all), 1)
        name = seat_of // (tile * copies)
        first_hot, second_hot = hot(first, name), hot(second, name)
        rank = jnp.dot((first_hot + second_hot).astype(BF16), before, preferred_element_type=F32)
        seat = (lax.rem(seat_of, tile) // cap == row_of // rows) & (rank == lax.rem(seat_of, cap).astype(F32))
        return first_hot, second_hot, seat

    first_hot, second_hot, seat = seats(experts * tile, 1)
    placed = jnp.where(seat, first_hot + second_hot, 0.0).astype(BF16)
    for i in range(2):
        picked = jnp.dot(placed, normed[keep + i], preferred_element_type=F32).astype(BF16)
        outgoing[:, i] = picked.reshape(experts, tile, q_width)
    both = pl.ds(keep, 2)
    home = pl.ds(pl.multiple_of((my_place * 2 + core) * group_rows + chip_x * tile, tile), tile)
    slots[both, home, :] = outgoing[chip // per_expert]

    pl.semaphore_wait(barrier, len(offsets) + 1 + inners - 1)

    for dy, dx in offsets:
        to = chip_at(dy, dx)
        remote(
            outgoing.at[to // per_expert], slots.at[both, home, :], out_sem.at[0], in_sem.at[my_place], to * 2 + core, z
        ).start()

    logits = nt_dot(router[...], normed_value)
    ids = lax.broadcasted_iota(jnp.int32, (experts, rows_all), 0)
    lead = jnp.sum(logits * hot(first, ids), axis=0, keepdims=True)
    trail = jnp.sum(logits * hot(second, ids), axis=0, keepdims=True)
    weight_a = 1.0 / (1.0 + jnp.exp(trail - lead))
    weight_b = 1.0 / (1.0 + jnp.exp(lead - trail))
    first_hot, second_hot, seat = seats(chips * tile, per_expert)
    mixing = jnp.transpose(jnp.where(seat, weight_a * first_hot + weight_b * second_hot, 0.0))
    mixing_high = mixing.astype(BF16)
    mix[:rows_all, :] = mixing_high
    mix[rows_all:, :] = (mixing - mixing_high.astype(F32)).astype(BF16)
    lane = 128
    base = pl.multiple_of(z * slice_width // lane * lane, lane)
    window = tokens[:, pl.ds(base, 2 * lane)].astype(F32)
    moved = pltpu.roll(window, 2 * lane - slice_width % lane, 1)
    residual[...] = jnp.where(z * slice_width == base, window, moved)[:, :slice_width]

    def rows_of(g, c):
        return pl.ds(pl.multiple_of((g * 2 + c) * group_rows, group_rows), group_rows)

    def group_of(g):
        return pl.ds(pl.multiple_of(g * group_rows, group_rows), group_rows)

    def swap_planes(j):
        g = place_of(lax.rem(chip_y + j, side))
        arrived = group_rows if j else group_rows - tile
        took(slots.at[both, pl.ds(0, arrived), :], in_sem.at[g])
        here = rows_of(g, core)
        for i in range(2):
            view = slots.at[keep + i, here, :]
            remote(view, view, deep_out_sem.at[0], deep_in_sem.at[i, g], section, deep_to[i]).start()
        view = slots.at[both, here, :]
        remote(view, view, share_out_sem.at[0], share_in_sem.at[0, g], partner, z).start()

    def share(j):
        g = place_of(lax.rem(chip_y + j, side))
        here = rows_of(g, core)
        for i in range(2):
            took(slots.at[pass_on + i, here, :], deep_in_sem.at[i, g])
        view = slots.at[pl.ds(pass_on, 2), here, :]
        remote(view, view, share_out_sem.at[0], share_in_sem.at[1, g], partner, z).start()

    def compute(j):
        pair = pl.multiple_of(lax.rem(chip_y + j, 2) * half_rows, half_rows)
        block = pl.ds(pair, half_rows)
        first_group = lax.rem(chip_y + j, 2) * (side // 2)
        for n in range(2):
            for m in range(side // 2):
                view = slots.at[pl.ds(0, 2), rows_of(first_group + m, 1 - core), :]
                took(view, share_in_sem.at[n, first_group + m])
        gate_up = nt_dot(slots[0, block, :], w_in_v[0])
        for q in range(1, 4):
            gate_up += nt_dot(slots[q, block, :], w_in_v[q])
        gate = gate_up[:, :hidden]
        active[block, :] = (gate / (1.0 + jnp.exp(-gate)) * gate_up[:, hidden:]).astype(BF16)
        for half, first_q in enumerate((pass_on, keep)):
            for i in range(2):
                partial[2 * half + i, block, :] = jnp.dot(
                    active[block, :], w_out_v[first_q + i], preferred_element_type=F32
                ).astype(BF16)
            for m in range(side // 2):
                g = first_group + m
                remote(
                    partial.at[pl.ds(2 * half, 2), rows_of(g, 1 - core), :],
                    pair_recv.at[pl.ds(2 * half, 2), group_of(g), :],
                    pair_out_sem.at[0],
                    pair_in_sem.at[half, g],
                    partner,
                    z,
                ).start()

    def fold(j):
        g = place_of(lax.rem(chip_y + j, side))
        here = group_of(g)
        took(pair_recv.at[pl.ds(0, 2), here, :], pair_in_sem.at[0, g])
        for i in range(2):
            total = partial[i, rows_of(g, core), :].astype(F32) + pair_recv[i, here, :].astype(F32)
            deep_send[i, here, :] = total.astype(BF16)
            remote(
                deep_send.at[i, here, :], deep_recv.at[i, here, :], fold_out_sem.at[0], fold_in_sem.at[i, g], section, fold_to[i]
            ).start()

    def give_back(j, i):
        g = place_of(lax.rem(chip_y + j, side))
        here = group_of(g)
        if i == 0:
            took(pair_recv.at[pl.ds(2, 2), here, :], pair_in_sem.at[1, g])
        took(deep_recv.at[i, here, :], fold_in_sem.at[i, g])
        total = partial[2 + i, rows_of(g, core), :].astype(F32) + pair_recv[2 + i, here, :].astype(F32)
        back_send[i, here, :] = (total + deep_recv[i, here, :].astype(F32)).astype(BF16)
        landing = pl.ds(pl.multiple_of(chip * tile, tile), tile)
        for dx in range(side):
            x = lax.rem(chip_x + dx, side)
            there = pl.ds(pl.multiple_of(g * group_rows + x * tile, tile), tile)
            if (j, dx) == (0, 0):
                back_recv[i, landing, :] = back_send[i, there, :]
            else:
                remote(
                    back_send.at[i, there, :],
                    back_recv.at[i, landing, :],
                    back_out_sem.at[0],
                    back_in_sem.at[i],
                    chip_at(j, dx) * 2 + core,
                    z,
                ).start()

    for q in range(4):
        took(w_in_v.at[q], w_sem.at[q])
        took(w_out_v.at[q], w_sem.at[4 + q])
    order_of_work = (
        (swap_planes, 0),
        (swap_planes, 1),
        (share, 0),
        (swap_planes, 2),
        (swap_planes, 3),
        (share, 1),
        (compute, 0),
        (share, 2),
        (fold, 0),
        (fold, 1),
        (share, 3),
        (compute, 2),
        (give_back, 0, 0),
        (give_back, 0, 1),
        (give_back, 1, 0),
        (give_back, 1, 1),
        (fold, 2),
        (fold, 3),
        (give_back, 2, 0),
        (give_back, 3, 0),
        (give_back, 2, 1),
        (give_back, 3, 1),
    )
    for work, *which in order_of_work:
        work(steps[which[0]], *which[1:])

    for i in range(2):
        took(back_recv.at[i, pl.ds(0, half_rows - tile), :], back_in_sem.at[i])
        parts = jnp.dot(mix[...], back_recv[i], preferred_element_type=F32)
        total = parts[:rows_all] + parts[rows_all:]
        for j in range(per_quarter):
            shifted = total if j == 0 else pltpu.roll(total, q_width - j * slice_width, 1)
            part_send[i * per_quarter + j] = shifted[:, :slice_width].astype(BF16)
        for away in sorted(range(inners), key=lambda d: -min(d, inners - d)):
            to = lax.rem(z + away, inners)

            @pl.when(to // per_quarter == keep + i)
            def _():
                n = lax.rem(to, inners // 2)
                if away == 0:
                    local(part_send.at[n], part_recv.at[z // 2], part_in_sem.at[0]).start()
                else:
                    remote(part_send.at[n], part_recv.at[z // 2], part_out_sem.at[0], part_in_sem.at[0], section, to).start()

    took(part_recv, part_in_sem.at[0])
    total = residual[...]
    for k in range(inners // 2):
        total += part_recv[k].astype(F32)
    out[...] = total.astype(BF16)

    took(back_send.at[:, pl.ds(0, half_rows - tile), :], out_sem.at[0])
    took(back_send, deep_out_sem.at[0])
    took(pair_recv, share_out_sem.at[0])
    took(pair_recv, pair_out_sem.at[0])
    took(deep_send, fold_out_sem.at[0])
    took(back_send.at[:, pl.ds(0, half_rows - tile), :], back_out_sem.at[0])
    inside = z // (inners // 2) == parity

    @pl.when(inside)
    def _():
        took(part_send.at[pl.ds(0, inners // 2 - 1)], part_out_sem.at[0])

    @pl.when(jnp.logical_not(inside))
    def _():
        took(part_send, part_out_sem.at[0])


def body(tokens, norm_gain, router, expert_in, expert_out, choices):
    sections = lax.axis_size("section")
    inners = lax.axis_size("inner")
    micro, rows, width = tokens.shape
    experts = router.shape[1]
    hidden = expert_in.shape[2]
    chips = sections // 2
    side = math.isqrt(chips)
    slice_width = width // inners
    q_width = width // 4
    rows_all = micro * rows
    tile = micro * (rows // 2)
    half_rows = chips * tile
    vmem = pl.BlockSpec(memory_space=pltpu.VMEM)
    anywhere = pl.BlockSpec(memory_space=pl.ANY)
    dma = pltpu.SemaphoreType.DMA
    moe = pl.pallas_call(
        functools.partial(moe_kernel, sections, inners, experts, micro),
        out_shape=jax.ShapeDtypeStruct((rows_all, slice_width), BF16),
        in_specs=[anywhere] * 6,
        out_specs=vmem,
        scratch_shapes=[
            pltpu.VMEM((rows_all, width), BF16),
            pltpu.VMEM((1, width), F32),
            pltpu.VMEM((experts, width), BF16),
            pltpu.VMEM((micro, 2, rows), jnp.int32),
            pltpu.VMEM((4, rows_all, q_width), BF16),
            pltpu.VMEM((experts, 2, tile, q_width), BF16),
            pltpu.VMEM((4, 2 * half_rows, q_width), BF16),
            pltpu.VMEM((4, 2 * hidden, q_width), BF16),
            pltpu.VMEM((4, hidden, q_width), BF16),
            pltpu.VMEM((2 * half_rows, hidden), BF16),
            pltpu.VMEM((2 * rows_all, half_rows), BF16),
            pltpu.VMEM((4, 2 * half_rows, q_width), BF16),
            pltpu.VMEM((4, half_rows, q_width), BF16),
            pltpu.VMEM((2, half_rows, q_width), BF16),
            pltpu.VMEM((2, half_rows, q_width), BF16),
            pltpu.VMEM((2, half_rows, q_width), BF16),
            pltpu.VMEM((2, half_rows, q_width), BF16),
            pltpu.VMEM((inners // 2, rows_all, slice_width), BF16),
            pltpu.VMEM((inners // 2, rows_all, slice_width), BF16),
            pltpu.VMEM((rows_all, slice_width), F32),
            dma((4,)),
            dma((8,)),
            dma((1,)),
            dma((side,)),
            dma((1,)),
            dma((2, side)),
            dma((1,)),
            dma((2, side)),
            dma((1,)),
            dma((2, side)),
            dma((1,)),
            dma((2, side)),
            dma((1,)),
            dma((2,)),
            dma((1,)),
            dma((1,)),
        ],
        compiler_params=pltpu.CompilerParams(
            collective_id=0, has_side_effects=True, vmem_limit_bytes=62 * 1024 * 1024
        ),
    )(
        tokens.reshape(rows_all, width),
        norm_gain.reshape(1, width),
        router.T,
        jnp.swapaxes(choices, 1, 2),
        expert_in.reshape(2 * hidden, width),
        expert_out.reshape(hidden, width),
    )
    return moe.reshape(micro, rows, slice_width)


def solution(mesh):
    return jax.shard_map(
        body,
        mesh=mesh,
        in_specs=(
            P(None, "section", None),
            P(),
            P(),
            P("section", None, "inner", None),
            P("section", "inner", None),
            P(None, "section", None),
        ),
        out_specs=P(None, "section", "inner"),
        check_vma=False,
    )
```

```python
import functools
import math

import jax
import jax.numpy as jnp
from jax import lax
from jax.experimental import pallas as pl
from jax.experimental.pallas import tpu as pltpu
from jax.sharding import PartitionSpec as P

epsilon = 1e-05
MESH = pl.DeviceIdType.MESH
BF16 = jnp.bfloat16
F32 = jnp.float32


def nt_dot(a, b):
    return lax.dot_general(a, b, (((1,), (1,)), ((), ())), preferred_element_type=F32)


def moe_kernel(
    sections,
    inners,
    experts,
    micro,
    tokens_hbm,
    gain_hbm,
    router_hbm,
    choices_hbm,
    w_in,
    w_out,
    out,
    tokens,
    gain,
    router,
    choices,
    normed,
    outgoing,
    slots,
    w_in_v,
    w_out_v,
    active,
    mix,
    partial,
    pair_recv,
    deep_send,
    deep_recv,
    back_send,
    back_recv,
    part_send,
    part_recv,
    residual,
    small_sem,
    w_sem,
    out_sem,
    in_sem,
    deep_out_sem,
    deep_in_sem,
    share_out_sem,
    share_in_sem,
    pair_out_sem,
    pair_in_sem,
    fold_out_sem,
    fold_in_sem,
    back_out_sem,
    back_in_sem,
    part_out_sem,
    part_in_sem,
):
    chips = sections // 2
    side = math.isqrt(chips)
    per_expert = chips // experts
    rows_all, width = tokens.shape
    rows = rows_all // micro
    cap = rows // 2
    tile = micro * cap
    q_width = width // 4
    hidden = w_out.shape[0]
    half_rows = chips * tile
    halves = side // 2
    batch = side // 2 * halves
    group_rows = 2 * tile
    slice_width = width // inners
    per_quarter = inners // 4

    section = lax.axis_index("section")
    z = lax.axis_index("inner")
    chip, core = section // 2, lax.rem(section, 2)
    chip_y, chip_x = chip // side, lax.rem(chip, side)
    parity = lax.rem(z, 2)
    z_up = lax.rem(z + 1, inners)
    z_down = lax.rem(z + inners - 1, inners)
    partner = chip * 2 + 1 - core
    deep_to = (z_up, z_down)
    fold_to = (z_down, z_up)
    keep = 2 * parity
    pass_on = 2 * (1 - parity)

    def local(src, dst, sem):
        return pltpu.make_async_copy(src, dst, sem)

    def remote(src, dst, send, recv, to_section, to_inner):
        return pltpu.make_async_remote_copy(
            src_ref=src, dst_ref=dst, send_sem=send, recv_sem=recv, device_id=(to_section, to_inner), device_id_type=MESH
        )

    def took(view, sem):
        local(view, view, sem).wait()

    small = ((tokens_hbm, tokens), (gain_hbm, gain), (router_hbm, router), (choices_hbm, choices))
    for n, (src, dst) in enumerate(small):
        local(src, dst, small_sem.at[n]).start()
    for q in range(4):
        local(w_in.at[:, pl.ds(q * q_width, q_width)], w_in_v.at[q], w_sem.at[q]).start()
    for q in range(4):
        local(w_out.at[:, pl.ds(q * q_width, q_width)], w_out_v.at[q], w_sem.at[4 + q]).start()

    steps = sorted(range(side), key=lambda j: (j % 2, j))

    chip_pair = chip_x // 2
    sibling = 1 - 2 * lax.rem(chip_x, 2)

    def group_at(j, h):
        y = lax.rem(chip_y + j, side)
        return (lax.rem(y, 2) * (side // 2) + y // 2) * halves + lax.rem(chip_pair + h, halves)

    def chips_at(j, h):
        y, x = lax.rem(chip_y + j, side), lax.rem(chip_x + 2 * h, side)
        return [(y * side + x + n * sibling, x + n * sibling) for n in range(2) if (j, h, n) != (0, 0, 0)]

    my_group = group_at(0, 0)

    barrier = pltpu.get_barrier_semaphore()
    for j in steps:
        for h in range(halves):
            for to, _ in chips_at(j, h):
                pl.semaphore_signal(barrier, inc=1, device_id=(to * 2 + core, z), device_id_type=MESH)
    pl.semaphore_signal(barrier, inc=1, device_id=(partner, z), device_id_type=MESH)
    for k in range(1, inners):
        pl.semaphore_signal(barrier, inc=1, device_id=(section, lax.rem(z + k, inners)), device_id_type=MESH)

    for n, (src, dst) in enumerate(small):
        local(src, dst, small_sem.at[n]).wait()
    values = tokens[...].astype(F32)
    inv_rms = lax.rsqrt(jnp.mean(values * values, axis=-1, keepdims=True) + epsilon)
    normed_value = (values * inv_rms * gain[...]).astype(BF16)
    for q in range(4):
        normed[q] = normed_value[:, q * q_width : (q + 1) * q_width]
    row_of = lax.broadcasted_iota(jnp.int32, (rows, rows_all), 0)
    col_of = lax.broadcasted_iota(jnp.int32, (rows, rows_all), 1)
    chosen = jnp.zeros((2, rows_all), F32)
    for m in range(micro):
        spread = jnp.where(col_of == row_of + m * rows, 1.0, 0.0).astype(BF16)
        chosen += jnp.dot(choices[m].astype(F32).astype(BF16), spread, preferred_element_type=F32)
    first, second = chosen[0:1].astype(jnp.int32), chosen[1:2].astype(jnp.int32)
    row_of = lax.broadcasted_iota(jnp.int32, (rows_all, rows_all), 0)
    col_of = lax.broadcasted_iota(jnp.int32, (rows_all, rows_all), 1)
    before = jnp.where((row_of // rows == col_of // rows) & (row_of < col_of), 1.0, 0.0).astype(BF16)

    def hot(index, name):
        return jnp.where(index == name, 1.0, 0.0).astype(F32)

    def seats(count, copies):
        seat_of = lax.broadcasted_iota(jnp.int32, (count, rows_all), 0)
        row_of = lax.broadcasted_iota(jnp.int32, (count, rows_all), 1)
        name = seat_of // (tile * copies)
        first_hot, second_hot = hot(first, name), hot(second, name)
        rank = jnp.dot((first_hot + second_hot).astype(BF16), before, preferred_element_type=F32)
        seat = (lax.rem(seat_of, tile) // cap == row_of // rows) & (rank == lax.rem(seat_of, cap).astype(F32))
        return first_hot, second_hot, seat

    first_hot, second_hot, seat = seats(experts * tile, 1)
    placed = jnp.where(seat, first_hot + second_hot, 0.0).astype(BF16)
    for i in range(2):
        picked = jnp.dot(placed, normed[keep + i], preferred_element_type=F32).astype(BF16)
        outgoing[:, i] = picked.reshape(experts, tile, q_width)
    both = pl.ds(keep, 2)
    home = pl.ds(pl.multiple_of((my_group * 2 + core) * group_rows + lax.rem(chip_x, 2) * tile, tile), tile)
    slots[both, home, :] = outgoing[chip // per_expert]

    pl.semaphore_wait(barrier, chips - 1 + 1 + inners - 1)

    for j in steps:
        for h in range(halves):
            for to, _ in chips_at(-j % side, h):
                remote(
                    outgoing.at[to // per_expert], slots.at[both, home, :], out_sem.at[0], in_sem.at[my_group], to * 2 + core, z
                ).start()

    logits = nt_dot(router[...], normed_value)
    ids = lax.broadcasted_iota(jnp.int32, (experts, rows_all), 0)
    lead = jnp.sum(logits * hot(first, ids), axis=0, keepdims=True)
    trail = jnp.sum(logits * hot(second, ids), axis=0, keepdims=True)
    weight_a = 1.0 / (1.0 + jnp.exp(trail - lead))
    weight_b = 1.0 / (1.0 + jnp.exp(lead - trail))
    first_hot, second_hot, seat = seats(chips * tile, per_expert)
    mixing = jnp.transpose(jnp.where(seat, weight_a * first_hot + weight_b * second_hot, 0.0))
    mixing_high = mixing.astype(BF16)
    mix[:rows_all, :] = mixing_high
    mix[rows_all:, :] = (mixing - mixing_high.astype(F32)).astype(BF16)
    lane = 128
    base = pl.multiple_of(z * slice_width // lane * lane, lane)
    window = tokens[:, pl.ds(base, 2 * lane)].astype(F32)
    moved = pltpu.roll(window, 2 * lane - slice_width % lane, 1)
    residual[...] = jnp.where(z * slice_width == base, window, moved)[:, :slice_width]

    def rows_of(g, c):
        return pl.ds(pl.multiple_of((g * 2 + c) * group_rows, group_rows), group_rows)

    def group_of(g):
        return pl.ds(pl.multiple_of(g * group_rows, group_rows), group_rows)

    def swap_planes(j, h):
        g = group_at(j, h)
        arrived = len(chips_at(j, h)) * tile
        took(slots.at[both, pl.ds(0, arrived), :], in_sem.at[g])
        here = rows_of(g, core)
        for i in range(2):
            view = slots.at[keep + i, here, :]
            remote(view, view, deep_out_sem.at[0], deep_in_sem.at[i, g], section, deep_to[i]).start()
        view = slots.at[both, here, :]
        remote(view, view, share_out_sem.at[0], share_in_sem.at[0, g], partner, z).start()

    def share(j, h):
        g = group_at(j, h)
        here = rows_of(g, core)
        for i in range(2):
            took(slots.at[pass_on + i, here, :], deep_in_sem.at[i, g])
        view = slots.at[pl.ds(pass_on, 2), here, :]
        remote(view, view, share_out_sem.at[0], share_in_sem.at[1, g], partner, z).start()

    def compute(j):
        pair = pl.multiple_of(lax.rem(chip_y + j, 2) * half_rows, half_rows)
        block = pl.ds(pair, half_rows)
        first_group = lax.rem(chip_y + j, 2) * batch
        for n in range(2):
            for m in range(batch):
                view = slots.at[pl.ds(0, 2), rows_of(first_group + m, 1 - core), :]
                took(view, share_in_sem.at[n, first_group + m])
        gate_up = nt_dot(slots[0, block, :], w_in_v[0])
        for q in range(1, 4):
            gate_up += nt_dot(slots[q, block, :], w_in_v[q])
        gate = gate_up[:, :hidden]
        active[block, :] = (gate / (1.0 + jnp.exp(-gate)) * gate_up[:, hidden:]).astype(BF16)
        for half, first_q in enumerate((pass_on, keep)):
            for i in range(2):
                partial[2 * half + i, block, :] = jnp.dot(
                    active[block, :], w_out_v[first_q + i], preferred_element_type=F32
                ).astype(BF16)
            for m in range(batch):
                g = first_group + m
                remote(
                    partial.at[pl.ds(2 * half, 2), rows_of(g, 1 - core), :],
                    pair_recv.at[pl.ds(2 * half, 2), group_of(g), :],
                    pair_out_sem.at[0],
                    pair_in_sem.at[half, g],
                    partner,
                    z,
                ).start()

    def fold(j, h):
        g = group_at(j, h)
        here = group_of(g)
        took(pair_recv.at[pl.ds(0, 2), here, :], pair_in_sem.at[0, g])
        for i in range(2):
            total = partial[i, rows_of(g, core), :].astype(F32) + pair_recv[i, here, :].astype(F32)
            deep_send[i, here, :] = total.astype(BF16)
            remote(
                deep_send.at[i, here, :], deep_recv.at[i, here, :], fold_out_sem.at[0], fold_in_sem.at[i, g], section, fold_to[i]
            ).start()

    def give_back(j, h, i):
        g = group_at(j, h)
        here = group_of(g)
        if i == 0:
            took(pair_recv.at[pl.ds(2, 2), here, :], pair_in_sem.at[1, g])
        took(deep_recv.at[i, here, :], fold_in_sem.at[i, g])
        total = partial[2 + i, rows_of(g, core), :].astype(F32) + pair_recv[2 + i, here, :].astype(F32)
        back_send[i, here, :] = (total + deep_recv[i, here, :].astype(F32)).astype(BF16)
        landing = pl.ds(pl.multiple_of(chip * tile, tile), tile)
        if (j, h) == (0, 0):
            there = pl.ds(pl.multiple_of(g * group_rows + lax.rem(chip_x, 2) * tile, tile), tile)
            back_recv[i, landing, :] = back_send[i, there, :]
        for to, x in chips_at(j, h):
            there = pl.ds(pl.multiple_of(g * group_rows + lax.rem(x, 2) * tile, tile), tile)
            remote(
                back_send.at[i, there, :],
                back_recv.at[i, landing, :],
                back_out_sem.at[0],
                back_in_sem.at[i],
                to * 2 + core,
                z,
            ).start()

    for q in range(4):
        took(w_in_v.at[q], w_sem.at[q])
        took(w_out_v.at[q], w_sem.at[4 + q])
    order_of_work = (
        (swap_planes, 0, 0),
        (swap_planes, 0, 1),
        (swap_planes, 1, 0),
        (swap_planes, 1, 1),
        (share, 0, 0),
        (share, 0, 1),
        (swap_planes, 2, 0),
        (swap_planes, 2, 1),
        (swap_planes, 3, 0),
        (swap_planes, 3, 1),
        (share, 1, 0),
        (share, 1, 1),
        (compute, 0),
        (share, 2, 0),
        (share, 2, 1),
        (fold, 0, 0),
        (fold, 0, 1),
        (fold, 1, 0),
        (fold, 1, 1),
        (share, 3, 0),
        (share, 3, 1),
        (compute, 2),
        (give_back, 0, 0, 0),
        (give_back, 0, 0, 1),
        (give_back, 0, 1, 0),
        (give_back, 0, 1, 1),
        (give_back, 1, 0, 0),
        (give_back, 1, 0, 1),
        (give_back, 1, 1, 0),
        (give_back, 1, 1, 1),
        (fold, 2, 0),
        (fold, 2, 1),
        (fold, 3, 0),
        (fold, 3, 1),
        (give_back, 2, 0, 0),
        (give_back, 2, 1, 0),
        (give_back, 3, 0, 0),
        (give_back, 3, 1, 0),
        (give_back, 2, 0, 1),
        (give_back, 2, 1, 1),
        (give_back, 3, 0, 1),
        (give_back, 3, 1, 1),
    )
    for work, k, *which in order_of_work:
        work(steps[k], *which)

    for i in range(2):
        took(back_recv.at[i, pl.ds(0, half_rows - tile), :], back_in_sem.at[i])
        parts = jnp.dot(mix[...], back_recv[i], preferred_element_type=F32)
        total = parts[:rows_all] + parts[rows_all:]
        for j in range(per_quarter):
            shifted = total if j == 0 else pltpu.roll(total, q_width - j * slice_width, 1)
            part_send[i * per_quarter + j] = shifted[:, :slice_width].astype(BF16)
        for away in sorted(range(inners), key=lambda d: -min(d, inners - d)):
            to = lax.rem(z + away, inners)

            @pl.when(to // per_quarter == keep + i)
            def _():
                n = lax.rem(to, inners // 2)
                if away == 0:
                    local(part_send.at[n], part_recv.at[z // 2], part_in_sem.at[0]).start()
                else:
                    remote(part_send.at[n], part_recv.at[z // 2], part_out_sem.at[0], part_in_sem.at[0], section, to).start()

    took(part_recv, part_in_sem.at[0])
    total = residual[...]
    for k in range(inners // 2):
        total += part_recv[k].astype(F32)
    out[...] = total.astype(BF16)

    took(back_send.at[:, pl.ds(0, half_rows - tile), :], out_sem.at[0])
    took(back_send, deep_out_sem.at[0])
    took(pair_recv, share_out_sem.at[0])
    took(pair_recv, pair_out_sem.at[0])
    took(deep_send, fold_out_sem.at[0])
    took(back_send.at[:, pl.ds(0, half_rows - tile), :], back_out_sem.at[0])
    inside = z // (inners // 2) == parity

    @pl.when(inside)
    def _():
        took(part_send.at[pl.ds(0, inners // 2 - 1)], part_out_sem.at[0])

    @pl.when(jnp.logical_not(inside))
    def _():
        took(part_send, part_out_sem.at[0])


def body(tokens, norm_gain, router, expert_in, expert_out, choices):
    sections = lax.axis_size("section")
    inners = lax.axis_size("inner")
    micro, rows, width = tokens.shape
    experts = router.shape[1]
    hidden = expert_in.shape[2]
    chips = sections // 2
    side = math.isqrt(chips)
    groups = side * (side // 2)
    slice_width = width // inners
    q_width = width // 4
    rows_all = micro * rows
    tile = micro * (rows // 2)
    half_rows = chips * tile
    vmem = pl.BlockSpec(memory_space=pltpu.VMEM)
    anywhere = pl.BlockSpec(memory_space=pl.ANY)
    dma = pltpu.SemaphoreType.DMA
    moe = pl.pallas_call(
        functools.partial(moe_kernel, sections, inners, experts, micro),
        out_shape=jax.ShapeDtypeStruct((rows_all, slice_width), BF16),
        in_specs=[anywhere] * 6,
        out_specs=vmem,
        scratch_shapes=[
            pltpu.VMEM((rows_all, width), BF16),
            pltpu.VMEM((1, width), F32),
            pltpu.VMEM((experts, width), BF16),
            pltpu.VMEM((micro, 2, rows), jnp.int32),
            pltpu.VMEM((4, rows_all, q_width), BF16),
            pltpu.VMEM((experts, 2, tile, q_width), BF16),
            pltpu.VMEM((4, 2 * half_rows, q_width), BF16),
            pltpu.VMEM((4, 2 * hidden, q_width), BF16),
            pltpu.VMEM((4, hidden, q_width), BF16),
            pltpu.VMEM((2 * half_rows, hidden), BF16),
            pltpu.VMEM((2 * rows_all, half_rows), BF16),
            pltpu.VMEM((4, 2 * half_rows, q_width), BF16),
            pltpu.VMEM((4, half_rows, q_width), BF16),
            pltpu.VMEM((2, half_rows, q_width), BF16),
            pltpu.VMEM((2, half_rows, q_width), BF16),
            pltpu.VMEM((2, half_rows, q_width), BF16),
            pltpu.VMEM((2, half_rows, q_width), BF16),
            pltpu.VMEM((inners // 2, rows_all, slice_width), BF16),
            pltpu.VMEM((inners // 2, rows_all, slice_width), BF16),
            pltpu.VMEM((rows_all, slice_width), F32),
            dma((4,)),
            dma((8,)),
            dma((1,)),
            dma((groups,)),
            dma((1,)),
            dma((2, groups)),
            dma((1,)),
            dma((2, groups)),
            dma((1,)),
            dma((2, groups)),
            dma((1,)),
            dma((2, groups)),
            dma((1,)),
            dma((2,)),
            dma((1,)),
            dma((1,)),
        ],
        compiler_params=pltpu.CompilerParams(
            collective_id=0, has_side_effects=True, vmem_limit_bytes=62 * 1024 * 1024
        ),
    )(
        tokens.reshape(rows_all, width),
        norm_gain.reshape(1, width),
        router.T,
        jnp.swapaxes(choices, 1, 2),
        expert_in.reshape(2 * hidden, width),
        expert_out.reshape(hidden, width),
    )
    return moe.reshape(micro, rows, slice_width)


def solution(mesh):
    return jax.shard_map(
        body,
        mesh=mesh,
        in_specs=(
            P(None, "section", None),
            P(),
            P(),
            P("section", None, "inner", None),
            P("section", "inner", None),
            P(None, "section", None),
        ),
        out_specs=P(None, "section", "inner"),
        check_vma=False,
    )
```

```python
import functools
import math

import jax
import jax.numpy as jnp
from jax import lax
from jax.experimental import pallas as pl
from jax.experimental.pallas import tpu as pltpu
from jax.sharding import PartitionSpec as P

epsilon = 1e-05
MESH = pl.DeviceIdType.MESH
BF16 = jnp.bfloat16
F32 = jnp.float32


def nt_dot(a, b):
    return lax.dot_general(a, b, (((1,), (1,)), ((), ())), preferred_element_type=F32)


def moe_kernel(
    sections,
    inners,
    experts,
    micro,
    tokens_hbm,
    gain_hbm,
    router_hbm,
    choices_hbm,
    w_in,
    w_out,
    out,
    tokens,
    gain,
    router,
    choices,
    normed,
    outgoing,
    slots,
    w_in_v,
    w_out_v,
    active,
    mix,
    partial,
    pair_recv,
    deep_send,
    deep_recv,
    back_send,
    back_recv,
    part_send,
    part_recv,
    residual,
    small_sem,
    w_sem,
    out_sem,
    in_sem,
    deep_out_sem,
    deep_in_sem,
    share_out_sem,
    share_in_sem,
    pair_out_sem,
    pair_in_sem,
    fold_out_sem,
    fold_in_sem,
    back_out_sem,
    back_in_sem,
    part_out_sem,
    part_in_sem,
    ready_sem,
):
    chips = sections // 2
    side = math.isqrt(chips)
    per_expert = chips // experts
    rows_all, width = tokens.shape
    rows = rows_all // micro
    cap = rows // 2
    tile = micro * cap
    q_width = width // 4
    hidden = w_out.shape[0]
    half_rows = chips * tile
    halves = side // 2
    batch = side // 2 * halves
    group_rows = 2 * tile
    slice_width = width // inners
    per_quarter = inners // 4

    section = lax.axis_index("section")
    z = lax.axis_index("inner")
    chip, core = section // 2, lax.rem(section, 2)
    chip_y, chip_x = chip // side, lax.rem(chip, side)
    parity = lax.rem(z, 2)
    z_up = lax.rem(z + 1, inners)
    z_down = lax.rem(z + inners - 1, inners)
    partner = chip * 2 + 1 - core
    deep_to = (z_up, z_down)
    fold_to = (z_down, z_up)
    keep = 2 * parity
    pass_on = 2 * (1 - parity)

    def local(src, dst, sem):
        return pltpu.make_async_copy(src, dst, sem)

    def remote(src, dst, send, recv, to_section, to_inner):
        return pltpu.make_async_remote_copy(
            src_ref=src, dst_ref=dst, send_sem=send, recv_sem=recv, device_id=(to_section, to_inner), device_id_type=MESH
        )

    def took(view, sem):
        local(view, view, sem).wait()

    small = ((tokens_hbm, tokens), (gain_hbm, gain), (router_hbm, router), (choices_hbm, choices))
    for n, (src, dst) in enumerate(small):
        local(src, dst, small_sem.at[n]).start()
    for q in range(4):
        local(w_in.at[:, pl.ds(q * q_width, q_width)], w_in_v.at[q], w_sem.at[q]).start()
    for q in range(4):
        local(w_out.at[:, pl.ds(q * q_width, q_width)], w_out_v.at[q], w_sem.at[4 + q]).start()

    steps = sorted(range(side), key=lambda j: (j % 2, j))

    chip_pair = chip_x // 2
    sibling = 1 - 2 * lax.rem(chip_x, 2)

    def group_at(j, h):
        y = lax.rem(chip_y + j, side)
        return (lax.rem(y, 2) * (side // 2) + y // 2) * halves + lax.rem(chip_pair + h, halves)

    def chips_at(j, h):
        y, x = lax.rem(chip_y + j, side), lax.rem(chip_x + 2 * h, side)
        return [(y * side + x + n * sibling, x + n * sibling) for n in range(2) if (j, h, n) != (0, 0, 0)]

    my_group = group_at(0, 0)

    barrier = pltpu.get_barrier_semaphore()
    for j in steps:
        for h in range(halves):
            for to, _ in chips_at(j, h):
                pl.semaphore_signal(barrier, inc=1, device_id=(to * 2 + core, z), device_id_type=MESH)
    pl.semaphore_signal(barrier, inc=1, device_id=(partner, z), device_id_type=MESH)
    for to in (z_up, z_down):
        pl.semaphore_signal(barrier, inc=1, device_id=(section, to), device_id_type=MESH)

    for n, (src, dst) in enumerate(small):
        local(src, dst, small_sem.at[n]).wait()
    values = tokens[...].astype(F32)
    inv_rms = lax.rsqrt(jnp.mean(values * values, axis=-1, keepdims=True) + epsilon)
    normed_value = (values * inv_rms * gain[...]).astype(BF16)
    for q in range(4):
        normed[q] = normed_value[:, q * q_width : (q + 1) * q_width]
    row_of = lax.broadcasted_iota(jnp.int32, (rows, rows_all), 0)
    col_of = lax.broadcasted_iota(jnp.int32, (rows, rows_all), 1)
    chosen = jnp.zeros((2, rows_all), F32)
    for m in range(micro):
        spread = jnp.where(col_of == row_of + m * rows, 1.0, 0.0).astype(BF16)
        chosen += jnp.dot(choices[m].astype(F32).astype(BF16), spread, preferred_element_type=F32)
    first, second = chosen[0:1].astype(jnp.int32), chosen[1:2].astype(jnp.int32)
    row_of = lax.broadcasted_iota(jnp.int32, (rows_all, rows_all), 0)
    col_of = lax.broadcasted_iota(jnp.int32, (rows_all, rows_all), 1)
    before = jnp.where((row_of // rows == col_of // rows) & (row_of < col_of), 1.0, 0.0).astype(BF16)

    def hot(index, name):
        return jnp.where(index == name, 1.0, 0.0).astype(F32)

    def seats(count, copies):
        seat_of = lax.broadcasted_iota(jnp.int32, (count, rows_all), 0)
        row_of = lax.broadcasted_iota(jnp.int32, (count, rows_all), 1)
        name = seat_of // (tile * copies)
        first_hot, second_hot = hot(first, name), hot(second, name)
        rank = jnp.dot((first_hot + second_hot).astype(BF16), before, preferred_element_type=F32)
        seat = (lax.rem(seat_of, tile) // cap == row_of // rows) & (rank == lax.rem(seat_of, cap).astype(F32))
        return first_hot, second_hot, seat

    first_hot, second_hot, seat = seats(experts * tile, 1)
    placed = jnp.where(seat, first_hot + second_hot, 0.0).astype(BF16)
    for i in range(2):
        picked = jnp.dot(placed, normed[keep + i], preferred_element_type=F32).astype(BF16)
        outgoing[:, i] = picked.reshape(experts, tile, q_width)
    both = pl.ds(keep, 2)
    home = pl.ds(pl.multiple_of((my_group * 2 + core) * group_rows + lax.rem(chip_x, 2) * tile, tile), tile)
    slots[both, home, :] = outgoing[chip // per_expert]

    pl.semaphore_wait(barrier, chips - 1 + 1 + 2)

    def tell_planes(n):
        for to in (lax.rem(z + 2**n, inners), lax.rem(z + inners - 2**n, inners)):
            pl.semaphore_signal(ready_sem.at[n], inc=1, device_id=(section, to), device_id_type=MESH)

    rounds = (inners // 2).bit_length() - 1
    tell_planes(0)

    for j in steps:
        for h in range(halves):
            for to, _ in chips_at(-j % side, h):
                remote(
                    outgoing.at[to // per_expert], slots.at[both, home, :], out_sem.at[0], in_sem.at[my_group], to * 2 + core, z
                ).start()

    logits = nt_dot(router[...], normed_value)
    ids = lax.broadcasted_iota(jnp.int32, (experts, rows_all), 0)
    lead = jnp.sum(logits * hot(first, ids), axis=0, keepdims=True)
    trail = jnp.sum(logits * hot(second, ids), axis=0, keepdims=True)
    weight_a = 1.0 / (1.0 + jnp.exp(trail - lead))
    weight_b = 1.0 / (1.0 + jnp.exp(lead - trail))
    first_hot, second_hot, seat = seats(chips * tile, per_expert)
    mixing = jnp.transpose(jnp.where(seat, weight_a * first_hot + weight_b * second_hot, 0.0))
    mixing_high = mixing.astype(BF16)
    mix[:rows_all, :] = mixing_high
    mix[rows_all:, :] = (mixing - mixing_high.astype(F32)).astype(BF16)
    lane = 128
    base = pl.multiple_of(z * slice_width // lane * lane, lane)
    window = tokens[:, pl.ds(base, 2 * lane)].astype(F32)
    moved = pltpu.roll(window, 2 * lane - slice_width % lane, 1)
    residual[...] = jnp.where(z * slice_width == base, window, moved)[:, :slice_width]

    def rows_of(g, c):
        return pl.ds(pl.multiple_of((g * 2 + c) * group_rows, group_rows), group_rows)

    def group_of(g):
        return pl.ds(pl.multiple_of(g * group_rows, group_rows), group_rows)

    def swap_planes(j, h):
        g = group_at(j, h)
        arrived = len(chips_at(j, h)) * tile
        took(slots.at[both, pl.ds(0, arrived), :], in_sem.at[g])
        here = rows_of(g, core)
        for i in range(2):
            view = slots.at[keep + i, here, :]
            remote(view, view, deep_out_sem.at[0], deep_in_sem.at[i, g], section, deep_to[i]).start()
        view = slots.at[both, here, :]
        remote(view, view, share_out_sem.at[0], share_in_sem.at[0, g], partner, z).start()

    def share(j, h):
        g = group_at(j, h)
        here = rows_of(g, core)
        for i in range(2):
            took(slots.at[pass_on + i, here, :], deep_in_sem.at[i, g])
        view = slots.at[pl.ds(pass_on, 2), here, :]
        remote(view, view, share_out_sem.at[0], share_in_sem.at[1, g], partner, z).start()

    def compute(j):
        pair = pl.multiple_of(lax.rem(chip_y + j, 2) * half_rows, half_rows)
        block = pl.ds(pair, half_rows)
        first_group = lax.rem(chip_y + j, 2) * batch
        for n in range(2):
            for m in range(batch):
                view = slots.at[pl.ds(0, 2), rows_of(first_group + m, 1 - core), :]
                took(view, share_in_sem.at[n, first_group + m])
        gate_up = nt_dot(slots[0, block, :], w_in_v[0])
        for q in range(1, 4):
            gate_up += nt_dot(slots[q, block, :], w_in_v[q])
        gate = gate_up[:, :hidden]
        active[block, :] = (gate / (1.0 + jnp.exp(-gate)) * gate_up[:, hidden:]).astype(BF16)
        for half, first_q in enumerate((pass_on, keep)):
            for i in range(2):
                partial[2 * half + i, block, :] = jnp.dot(
                    active[block, :], w_out_v[first_q + i], preferred_element_type=F32
                ).astype(BF16)
            for m in range(batch):
                g = first_group + m
                remote(
                    partial.at[pl.ds(2 * half, 2), rows_of(g, 1 - core), :],
                    pair_recv.at[pl.ds(2 * half, 2), group_of(g), :],
                    pair_out_sem.at[0],
                    pair_in_sem.at[half, g],
                    partner,
                    z,
                ).start()

    def fold(j, h):
        g = group_at(j, h)
        here = group_of(g)
        took(pair_recv.at[pl.ds(0, 2), here, :], pair_in_sem.at[0, g])
        for i in range(2):
            total = partial[i, rows_of(g, core), :].astype(F32) + pair_recv[i, here, :].astype(F32)
            deep_send[i, here, :] = total.astype(BF16)
            remote(
                deep_send.at[i, here, :], deep_recv.at[i, here, :], fold_out_sem.at[0], fold_in_sem.at[i, g], section, fold_to[i]
            ).start()

    def give_back(j, h, i):
        g = group_at(j, h)
        here = group_of(g)
        if i == 0:
            took(pair_recv.at[pl.ds(2, 2), here, :], pair_in_sem.at[1, g])
        took(deep_recv.at[i, here, :], fold_in_sem.at[i, g])
        total = partial[2 + i, rows_of(g, core), :].astype(F32) + pair_recv[2 + i, here, :].astype(F32)
        back_send[i, here, :] = (total + deep_recv[i, here, :].astype(F32)).astype(BF16)
        landing = pl.ds(pl.multiple_of(chip * tile, tile), tile)
        if (j, h) == (0, 0):
            there = pl.ds(pl.multiple_of(g * group_rows + lax.rem(chip_x, 2) * tile, tile), tile)
            back_recv[i, landing, :] = back_send[i, there, :]
        for to, x in chips_at(j, h):
            there = pl.ds(pl.multiple_of(g * group_rows + lax.rem(x, 2) * tile, tile), tile)
            remote(
                back_send.at[i, there, :],
                back_recv.at[i, landing, :],
                back_out_sem.at[0],
                back_in_sem.at[i],
                to * 2 + core,
                z,
            ).start()

    for q in range(4):
        took(w_in_v.at[q], w_sem.at[q])
        took(w_out_v.at[q], w_sem.at[4 + q])
    order_of_work = (
        (swap_planes, 0, 0),
        (swap_planes, 0, 1),
        (swap_planes, 1, 0),
        (swap_planes, 1, 1),
        (share, 0, 0),
        (share, 0, 1),
        (swap_planes, 2, 0),
        (swap_planes, 2, 1),
        (swap_planes, 3, 0),
        (swap_planes, 3, 1),
        (share, 1, 0),
        (share, 1, 1),
        (compute, 0),
        (share, 2, 0),
        (share, 2, 1),
        (fold, 0, 0),
        (fold, 0, 1),
        (fold, 1, 0),
        (fold, 1, 1),
        (share, 3, 0),
        (share, 3, 1),
        (compute, 2),
        (give_back, 0, 0, 0),
        (give_back, 0, 0, 1),
        (give_back, 0, 1, 0),
        (give_back, 0, 1, 1),
        (give_back, 1, 0, 0),
        (give_back, 1, 0, 1),
        (give_back, 1, 1, 0),
        (give_back, 1, 1, 1),
        (fold, 2, 0),
        (fold, 2, 1),
        (fold, 3, 0),
        (fold, 3, 1),
        (give_back, 2, 0, 0),
        (give_back, 2, 1, 0),
        (give_back, 3, 0, 0),
        (give_back, 3, 1, 0),
        (give_back, 2, 0, 1),
        (give_back, 2, 1, 1),
        (give_back, 3, 0, 1),
        (give_back, 3, 1, 1),
    )
    told = 0
    for n, (work, k, *which) in enumerate(order_of_work):
        work(steps[k], *which)
        if n in (3, 9) and told < rounds - 1:
            pl.semaphore_wait(ready_sem.at[told], 2)
            told += 1
            tell_planes(told)

    pl.semaphore_wait(ready_sem.at[rounds - 1], 2)
    for i in range(2):
        took(back_recv.at[i, pl.ds(0, half_rows - tile), :], back_in_sem.at[i])
        parts = jnp.dot(mix[...], back_recv[i], preferred_element_type=F32)
        total = parts[:rows_all] + parts[rows_all:]
        for j in range(per_quarter):
            shifted = total if j == 0 else pltpu.roll(total, q_width - j * slice_width, 1)
            part_send[i * per_quarter + j] = shifted[:, :slice_width].astype(BF16)
        for away in sorted(range(inners), key=lambda d: -min(d, inners - d)):
            to = lax.rem(z + away, inners)

            @pl.when(to // per_quarter == keep + i)
            def _():
                n = lax.rem(to, inners // 2)
                if away == 0:
                    local(part_send.at[n], part_recv.at[z // 2], part_in_sem.at[0]).start()
                else:
                    remote(part_send.at[n], part_recv.at[z // 2], part_out_sem.at[0], part_in_sem.at[0], section, to).start()

    took(part_recv, part_in_sem.at[0])
    total = residual[...]
    for k in range(inners // 2):
        total += part_recv[k].astype(F32)
    out[...] = total.astype(BF16)

    took(back_send.at[:, pl.ds(0, half_rows - tile), :], out_sem.at[0])
    took(back_send, deep_out_sem.at[0])
    took(pair_recv, share_out_sem.at[0])
    took(pair_recv, pair_out_sem.at[0])
    took(deep_send, fold_out_sem.at[0])
    took(back_send.at[:, pl.ds(0, half_rows - tile), :], back_out_sem.at[0])
    inside = z // (inners // 2) == parity

    @pl.when(inside)
    def _():
        took(part_send.at[pl.ds(0, inners // 2 - 1)], part_out_sem.at[0])

    @pl.when(jnp.logical_not(inside))
    def _():
        took(part_send, part_out_sem.at[0])


def body(tokens, norm_gain, router, expert_in, expert_out, choices):
    sections = lax.axis_size("section")
    inners = lax.axis_size("inner")
    micro, rows, width = tokens.shape
    experts = router.shape[1]
    hidden = expert_in.shape[2]
    chips = sections // 2
    side = math.isqrt(chips)
    groups = side * (side // 2)
    slice_width = width // inners
    q_width = width // 4
    rows_all = micro * rows
    tile = micro * (rows // 2)
    half_rows = chips * tile
    vmem = pl.BlockSpec(memory_space=pltpu.VMEM)
    anywhere = pl.BlockSpec(memory_space=pl.ANY)
    dma = pltpu.SemaphoreType.DMA
    moe = pl.pallas_call(
        functools.partial(moe_kernel, sections, inners, experts, micro),
        out_shape=jax.ShapeDtypeStruct((rows_all, slice_width), BF16),
        in_specs=[anywhere] * 6,
        out_specs=vmem,
        scratch_shapes=[
            pltpu.VMEM((rows_all, width), BF16),
            pltpu.VMEM((1, width), F32),
            pltpu.VMEM((experts, width), BF16),
            pltpu.VMEM((micro, 2, rows), jnp.int32),
            pltpu.VMEM((4, rows_all, q_width), BF16),
            pltpu.VMEM((experts, 2, tile, q_width), BF16),
            pltpu.VMEM((4, 2 * half_rows, q_width), BF16),
            pltpu.VMEM((4, 2 * hidden, q_width), BF16),
            pltpu.VMEM((4, hidden, q_width), BF16),
            pltpu.VMEM((2 * half_rows, hidden), BF16),
            pltpu.VMEM((2 * rows_all, half_rows), BF16),
            pltpu.VMEM((4, 2 * half_rows, q_width), BF16),
            pltpu.VMEM((4, half_rows, q_width), BF16),
            pltpu.VMEM((2, half_rows, q_width), BF16),
            pltpu.VMEM((2, half_rows, q_width), BF16),
            pltpu.VMEM((2, half_rows, q_width), BF16),
            pltpu.VMEM((2, half_rows, q_width), BF16),
            pltpu.VMEM((inners // 2, rows_all, slice_width), BF16),
            pltpu.VMEM((inners // 2, rows_all, slice_width), BF16),
            pltpu.VMEM((rows_all, slice_width), F32),
            dma((4,)),
            dma((8,)),
            dma((1,)),
            dma((groups,)),
            dma((1,)),
            dma((2, groups)),
            dma((1,)),
            dma((2, groups)),
            dma((1,)),
            dma((2, groups)),
            dma((1,)),
            dma((2, groups)),
            dma((1,)),
            dma((2,)),
            dma((1,)),
            dma((1,)),
            pltpu.SemaphoreType.REGULAR(((inners // 2).bit_length() - 1,)),
        ],
        compiler_params=pltpu.CompilerParams(
            collective_id=0, has_side_effects=True, vmem_limit_bytes=62 * 1024 * 1024
        ),
    )(
        tokens.reshape(rows_all, width),
        norm_gain.reshape(1, width),
        router.T,
        jnp.swapaxes(choices, 1, 2),
        expert_in.reshape(2 * hidden, width),
        expert_out.reshape(hidden, width),
    )
    return moe.reshape(micro, rows, slice_width)


def solution(mesh):
    return jax.shard_map(
        body,
        mesh=mesh,
        in_specs=(
            P(None, "section", None),
            P(),
            P(),
            P("section", None, "inner", None),
            P("section", "inner", None),
            P(None, "section", None),
        ),
        out_specs=P(None, "section", "inner"),
        check_vma=False,
    )
```

```python
import functools
import math

import jax
import jax.numpy as jnp
from jax import lax
from jax.experimental import pallas as pl
from jax.experimental.pallas import tpu as pltpu
from jax.sharding import PartitionSpec as P

epsilon = 1e-05
MESH = pl.DeviceIdType.MESH
BF16 = jnp.bfloat16
F32 = jnp.float32


def nt_dot(a, b):
    return lax.dot_general(a, b, (((1,), (1,)), ((), ())), preferred_element_type=F32)


def moe_kernel(
    sections,
    inners,
    experts,
    micro,
    tokens_hbm,
    gain_hbm,
    router_hbm,
    choices_hbm,
    w_in,
    w_out,
    out,
    tokens,
    gain,
    router,
    choices,
    normed,
    outgoing,
    slots,
    w_in_v,
    w_out_v,
    active,
    mix,
    partial,
    pair_recv,
    deep_send,
    deep_recv,
    back_send,
    back_recv,
    part_send,
    part_recv,
    residual,
    small_sem,
    w_sem,
    out_sem,
    in_sem,
    deep_out_sem,
    deep_in_sem,
    share_out_sem,
    share_in_sem,
    pair_out_sem,
    pair_in_sem,
    fold_out_sem,
    fold_in_sem,
    back_out_sem,
    back_in_sem,
    part_out_sem,
    part_in_sem,
    ready_sem,
):
    chips = sections // 2
    side = math.isqrt(chips)
    per_expert = chips // experts
    rows_all, width = tokens.shape
    rows = rows_all // micro
    cap = rows // 2
    tile = micro * cap
    q_width = width // 4
    hidden = w_out.shape[0]
    half_rows = chips * tile
    halves = side // 2
    batch = side // 2 * halves
    group_rows = 2 * tile
    slice_width = width // inners
    per_quarter = inners // 4

    section = lax.axis_index("section")
    z = lax.axis_index("inner")
    chip, core = section // 2, lax.rem(section, 2)
    chip_y, chip_x = chip // side, lax.rem(chip, side)
    parity = lax.rem(z, 2)
    z_up = lax.rem(z + 1, inners)
    z_down = lax.rem(z + inners - 1, inners)
    partner = chip * 2 + 1 - core
    deep_to = (z_up, z_down)
    fold_to = (z_down, z_up)
    keep = 2 * parity
    pass_on = 2 * (1 - parity)

    def local(src, dst, sem):
        return pltpu.make_async_copy(src, dst, sem)

    def remote(src, dst, send, recv, to_section, to_inner):
        return pltpu.make_async_remote_copy(
            src_ref=src, dst_ref=dst, send_sem=send, recv_sem=recv, device_id=(to_section, to_inner), device_id_type=MESH
        )

    def took(view, sem):
        local(view, view, sem).wait()

    small = ((tokens_hbm, tokens), (gain_hbm, gain), (router_hbm, router), (choices_hbm, choices))
    for n, (src, dst) in enumerate(small):
        local(src, dst, small_sem.at[n]).start()
    for q in range(4):
        local(w_in.at[:, pl.ds(q * q_width, q_width)], w_in_v.at[q], w_sem.at[q]).start()
    for q in range(4):
        local(w_out.at[:, pl.ds(q * q_width, q_width)], w_out_v.at[q], w_sem.at[4 + q]).start()

    steps = sorted(range(side), key=lambda j: (j % 2, j))

    chip_pair = chip_x // 2
    sibling = 1 - 2 * lax.rem(chip_x, 2)

    def group_at(j, h):
        y = lax.rem(chip_y + j, side)
        return (lax.rem(y, 2) * (side // 2) + y // 2) * halves + lax.rem(chip_pair + h, halves)

    def chips_at(j, h):
        y, x = lax.rem(chip_y + j, side), lax.rem(chip_x + 2 * h, side)
        return [(y * side + x + n * sibling, x + n * sibling) for n in range(2) if (j, h, n) != (0, 0, 0)]

    my_group = group_at(0, 0)

    barrier = pltpu.get_barrier_semaphore()
    for to in (z_up, z_down):
        pl.semaphore_signal(barrier, inc=1, device_id=(section, to), device_id_type=MESH)
    for j in steps:
        for h in range(halves):
            for to, _ in chips_at(j, h):
                pl.semaphore_signal(barrier, inc=1, device_id=(to * 2 + core, z), device_id_type=MESH)
    pl.semaphore_signal(barrier, inc=1, device_id=(partner, z), device_id_type=MESH)

    for n, (src, dst) in enumerate(small):
        local(src, dst, small_sem.at[n]).wait()
    values = tokens[...].astype(F32)
    inv_rms = lax.rsqrt(jnp.mean(values * values, axis=-1, keepdims=True) + epsilon)
    normed_value = (values * inv_rms * gain[...]).astype(BF16)
    for q in range(4):
        normed[q] = normed_value[:, q * q_width : (q + 1) * q_width]
    row_of = lax.broadcasted_iota(jnp.int32, (rows, rows_all), 0)
    col_of = lax.broadcasted_iota(jnp.int32, (rows, rows_all), 1)
    chosen = jnp.zeros((2, rows_all), F32)
    for m in range(micro):
        spread = jnp.where(col_of == row_of + m * rows, 1.0, 0.0).astype(BF16)
        chosen += jnp.dot(choices[m].astype(F32).astype(BF16), spread, preferred_element_type=F32)
    first, second = chosen[0:1].astype(jnp.int32), chosen[1:2].astype(jnp.int32)
    row_of = lax.broadcasted_iota(jnp.int32, (rows_all, rows_all), 0)
    col_of = lax.broadcasted_iota(jnp.int32, (rows_all, rows_all), 1)
    before = jnp.where((row_of // rows == col_of // rows) & (row_of < col_of), 1.0, 0.0).astype(BF16)

    def hot(index, name):
        return jnp.where(index == name, 1.0, 0.0).astype(F32)

    def seats(count, copies):
        seat_of = lax.broadcasted_iota(jnp.int32, (count, rows_all), 0)
        row_of = lax.broadcasted_iota(jnp.int32, (count, rows_all), 1)
        name = seat_of // (tile * copies)
        first_hot, second_hot = hot(first, name), hot(second, name)
        rank = jnp.dot((first_hot + second_hot).astype(BF16), before, preferred_element_type=F32)
        seat = (lax.rem(seat_of, tile) // cap == row_of // rows) & (rank == lax.rem(seat_of, cap).astype(F32))
        return first_hot, second_hot, seat

    first_hot, second_hot, seat = seats(experts * tile, 1)
    placed = jnp.where(seat, first_hot + second_hot, 0.0).astype(BF16)
    for i in range(2):
        picked = jnp.dot(placed, normed[keep + i], preferred_element_type=F32).astype(BF16)
        outgoing[:, i] = picked.reshape(experts, tile, q_width)
    both = pl.ds(keep, 2)
    home = pl.ds(pl.multiple_of((my_group * 2 + core) * group_rows + lax.rem(chip_x, 2) * tile, tile), tile)
    slots[both, home, :] = outgoing[chip // per_expert]

    pl.semaphore_wait(barrier, chips - 1 + 1 + 2)

    def tell_planes(n):
        for to in (lax.rem(z + 2**n, inners), lax.rem(z + inners - 2**n, inners)):
            pl.semaphore_signal(ready_sem.at[n], inc=1, device_id=(section, to), device_id_type=MESH)

    rounds = (inners // 2).bit_length() - 1
    tell_planes(0)

    for j in steps:
        for h in range(halves):
            for to, _ in chips_at(-j % side, h):
                remote(
                    outgoing.at[to // per_expert], slots.at[both, home, :], out_sem.at[0], in_sem.at[my_group], to * 2 + core, z
                ).start()

    logits = nt_dot(router[...], normed_value)
    ids = lax.broadcasted_iota(jnp.int32, (experts, rows_all), 0)
    lead = jnp.sum(logits * hot(first, ids), axis=0, keepdims=True)
    trail = jnp.sum(logits * hot(second, ids), axis=0, keepdims=True)
    weight_a = 1.0 / (1.0 + jnp.exp(trail - lead))
    weight_b = 1.0 / (1.0 + jnp.exp(lead - trail))
    first_hot, second_hot, seat = seats(chips * tile, per_expert)
    mixing = jnp.transpose(jnp.where(seat, weight_a * first_hot + weight_b * second_hot, 0.0))
    mixing_high = mixing.astype(BF16)
    mix[:rows_all, :] = mixing_high
    mix[rows_all:, :] = (mixing - mixing_high.astype(F32)).astype(BF16)
    lane = 128
    base = pl.multiple_of(z * slice_width // lane * lane, lane)
    window = tokens[:, pl.ds(base, 2 * lane)].astype(F32)
    moved = pltpu.roll(window, 2 * lane - slice_width % lane, 1)
    residual[...] = jnp.where(z * slice_width == base, window, moved)[:, :slice_width]

    def rows_of(g, c):
        return pl.ds(pl.multiple_of((g * 2 + c) * group_rows, group_rows), group_rows)

    def group_of(g):
        return pl.ds(pl.multiple_of(g * group_rows, group_rows), group_rows)

    def swap_planes(j, h):
        g = group_at(j, h)
        arrived = len(chips_at(j, h)) * tile
        took(slots.at[both, pl.ds(0, arrived), :], in_sem.at[g])
        here = rows_of(g, core)
        for i in range(2):
            view = slots.at[keep + i, here, :]
            remote(view, view, deep_out_sem.at[0], deep_in_sem.at[i, g], section, deep_to[i]).start()
        view = slots.at[both, here, :]
        remote(view, view, share_out_sem.at[0], share_in_sem.at[0, g], partner, z).start()

    def share(j, h):
        g = group_at(j, h)
        here = rows_of(g, core)
        for i in range(2):
            took(slots.at[pass_on + i, here, :], deep_in_sem.at[i, g])
        view = slots.at[pl.ds(pass_on, 2), here, :]
        remote(view, view, share_out_sem.at[0], share_in_sem.at[1, g], partner, z).start()

    def compute(j):
        pair = pl.multiple_of(lax.rem(chip_y + j, 2) * half_rows, half_rows)
        block = pl.ds(pair, half_rows)
        first_group = lax.rem(chip_y + j, 2) * batch
        for n in range(2):
            for m in range(batch):
                view = slots.at[pl.ds(0, 2), rows_of(first_group + m, 1 - core), :]
                took(view, share_in_sem.at[n, first_group + m])
        gate_up = nt_dot(slots[0, block, :], w_in_v[0])
        for q in range(1, 4):
            gate_up += nt_dot(slots[q, block, :], w_in_v[q])
        gate = gate_up[:, :hidden]
        active[block, :] = (gate / (1.0 + jnp.exp(-gate)) * gate_up[:, hidden:]).astype(BF16)
        for half, first_q in enumerate((pass_on, keep)):
            for i in range(2):
                partial[2 * half + i, block, :] = jnp.dot(
                    active[block, :], w_out_v[first_q + i], preferred_element_type=F32
                ).astype(BF16)
            for m in range(batch):
                g = first_group + m
                remote(
                    partial.at[pl.ds(2 * half, 2), rows_of(g, 1 - core), :],
                    pair_recv.at[pl.ds(2 * half, 2), group_of(g), :],
                    pair_out_sem.at[0],
                    pair_in_sem.at[half, g],
                    partner,
                    z,
                ).start()

    def fold(j, h):
        g = group_at(j, h)
        here = group_of(g)
        took(pair_recv.at[pl.ds(0, 2), here, :], pair_in_sem.at[0, g])
        for i in range(2):
            total = partial[i, rows_of(g, core), :].astype(F32) + pair_recv[i, here, :].astype(F32)
            deep_send[i, here, :] = total.astype(BF16)
            remote(
                deep_send.at[i, here, :], deep_recv.at[i, here, :], fold_out_sem.at[0], fold_in_sem.at[i, g], section, fold_to[i]
            ).start()

    def give_back(j, h, i):
        g = group_at(j, h)
        here = group_of(g)
        if i == 0:
            took(pair_recv.at[pl.ds(2, 2), here, :], pair_in_sem.at[1, g])
        took(deep_recv.at[i, here, :], fold_in_sem.at[i, g])
        total = partial[2 + i, rows_of(g, core), :].astype(F32) + pair_recv[2 + i, here, :].astype(F32)
        back_send[i, here, :] = (total + deep_recv[i, here, :].astype(F32)).astype(BF16)
        landing = pl.ds(pl.multiple_of(chip * tile, tile), tile)
        if (j, h) == (0, 0):
            there = pl.ds(pl.multiple_of(g * group_rows + lax.rem(chip_x, 2) * tile, tile), tile)
            back_recv[i, landing, :] = back_send[i, there, :]
        for to, x in chips_at(j, h):
            there = pl.ds(pl.multiple_of(g * group_rows + lax.rem(x, 2) * tile, tile), tile)
            remote(
                back_send.at[i, there, :],
                back_recv.at[i, landing, :],
                back_out_sem.at[0],
                back_in_sem.at[i],
                to * 2 + core,
                z,
            ).start()

    for q in range(4):
        took(w_in_v.at[q], w_sem.at[q])
        took(w_out_v.at[q], w_sem.at[4 + q])
    order_of_work = (
        (swap_planes, 0, 0),
        (swap_planes, 0, 1),
        (swap_planes, 1, 0),
        (swap_planes, 1, 1),
        (share, 0, 0),
        (share, 0, 1),
        (swap_planes, 2, 0),
        (swap_planes, 2, 1),
        (swap_planes, 3, 0),
        (swap_planes, 3, 1),
        (share, 1, 0),
        (share, 1, 1),
        (compute, 0),
        (share, 2, 0),
        (share, 2, 1),
        (fold, 0, 0),
        (fold, 0, 1),
        (fold, 1, 0),
        (fold, 1, 1),
        (share, 3, 0),
        (share, 3, 1),
        (compute, 2),
        (give_back, 0, 0, 0),
        (give_back, 0, 0, 1),
        (give_back, 0, 1, 0),
        (give_back, 0, 1, 1),
        (give_back, 1, 0, 0),
        (give_back, 1, 0, 1),
        (give_back, 1, 1, 0),
        (give_back, 1, 1, 1),
        (fold, 2, 0),
        (fold, 2, 1),
        (fold, 3, 0),
        (fold, 3, 1),
        (give_back, 2, 0, 0),
        (give_back, 2, 1, 0),
        (give_back, 3, 0, 0),
        (give_back, 3, 1, 0),
        (give_back, 2, 0, 1),
        (give_back, 2, 1, 1),
        (give_back, 3, 0, 1),
        (give_back, 3, 1, 1),
    )
    told = 0
    for n, (work, k, *which) in enumerate(order_of_work):
        work(steps[k], *which)
        if n in (1, 5) and told < rounds - 1:
            pl.semaphore_wait(ready_sem.at[told], 2)
            told += 1
            tell_planes(told)

    pl.semaphore_wait(ready_sem.at[rounds - 1], 2)
    for i in range(2):
        took(back_recv.at[i, pl.ds(0, half_rows - tile), :], back_in_sem.at[i])
        parts = jnp.dot(mix[...], back_recv[i], preferred_element_type=F32)
        total = parts[:rows_all] + parts[rows_all:]
        for j in range(per_quarter):
            shifted = total if j == 0 else pltpu.roll(total, q_width - j * slice_width, 1)
            part_send[i * per_quarter + j] = shifted[:, :slice_width].astype(BF16)
        for away in sorted(range(inners), key=lambda d: -min(d, inners - d)):
            to = lax.rem(z + away, inners)

            @pl.when(to // per_quarter == keep + i)
            def _():
                n = lax.rem(to, inners // 2)
                if away == 0:
                    local(part_send.at[n], part_recv.at[z // 2], part_in_sem.at[0]).start()
                else:
                    remote(part_send.at[n], part_recv.at[z // 2], part_out_sem.at[0], part_in_sem.at[0], section, to).start()

    took(part_recv, part_in_sem.at[0])
    total = residual[...]
    for k in range(inners // 2):
        total += part_recv[k].astype(F32)
    out[...] = total.astype(BF16)

    took(back_send.at[:, pl.ds(0, half_rows - tile), :], out_sem.at[0])
    took(back_send, deep_out_sem.at[0])
    took(pair_recv, share_out_sem.at[0])
    took(pair_recv, pair_out_sem.at[0])
    took(deep_send, fold_out_sem.at[0])
    took(back_send.at[:, pl.ds(0, half_rows - tile), :], back_out_sem.at[0])
    inside = z // (inners // 2) == parity

    @pl.when(inside)
    def _():
        took(part_send.at[pl.ds(0, inners // 2 - 1)], part_out_sem.at[0])

    @pl.when(jnp.logical_not(inside))
    def _():
        took(part_send, part_out_sem.at[0])


def body(tokens, norm_gain, router, expert_in, expert_out, choices):
    sections = lax.axis_size("section")
    inners = lax.axis_size("inner")
    micro, rows, width = tokens.shape
    experts = router.shape[1]
    hidden = expert_in.shape[2]
    chips = sections // 2
    side = math.isqrt(chips)
    groups = side * (side // 2)
    slice_width = width // inners
    q_width = width // 4
    rows_all = micro * rows
    tile = micro * (rows // 2)
    half_rows = chips * tile
    vmem = pl.BlockSpec(memory_space=pltpu.VMEM)
    anywhere = pl.BlockSpec(memory_space=pl.ANY)
    dma = pltpu.SemaphoreType.DMA
    moe = pl.pallas_call(
        functools.partial(moe_kernel, sections, inners, experts, micro),
        out_shape=jax.ShapeDtypeStruct((rows_all, slice_width), BF16),
        in_specs=[anywhere] * 6,
        out_specs=vmem,
        scratch_shapes=[
            pltpu.VMEM((rows_all, width), BF16),
            pltpu.VMEM((1, width), F32),
            pltpu.VMEM((experts, width), BF16),
            pltpu.VMEM((micro, 2, rows), jnp.int32),
            pltpu.VMEM((4, rows_all, q_width), BF16),
            pltpu.VMEM((experts, 2, tile, q_width), BF16),
            pltpu.VMEM((4, 2 * half_rows, q_width), BF16),
            pltpu.VMEM((4, 2 * hidden, q_width), BF16),
            pltpu.VMEM((4, hidden, q_width), BF16),
            pltpu.VMEM((2 * half_rows, hidden), BF16),
            pltpu.VMEM((2 * rows_all, half_rows), BF16),
            pltpu.VMEM((4, 2 * half_rows, q_width), BF16),
            pltpu.VMEM((4, half_rows, q_width), BF16),
            pltpu.VMEM((2, half_rows, q_width), BF16),
            pltpu.VMEM((2, half_rows, q_width), BF16),
            pltpu.VMEM((2, half_rows, q_width), BF16),
            pltpu.VMEM((2, half_rows, q_width), BF16),
            pltpu.VMEM((inners // 2, rows_all, slice_width), BF16),
            pltpu.VMEM((inners // 2, rows_all, slice_width), BF16),
            pltpu.VMEM((rows_all, slice_width), F32),
            dma((4,)),
            dma((8,)),
            dma((1,)),
            dma((groups,)),
            dma((1,)),
            dma((2, groups)),
            dma((1,)),
            dma((2, groups)),
            dma((1,)),
            dma((2, groups)),
            dma((1,)),
            dma((2, groups)),
            dma((1,)),
            dma((2,)),
            dma((1,)),
            dma((1,)),
            pltpu.SemaphoreType.REGULAR(((inners // 2).bit_length() - 1,)),
        ],
        compiler_params=pltpu.CompilerParams(
            collective_id=0, has_side_effects=True, vmem_limit_bytes=62 * 1024 * 1024
        ),
    )(
        tokens.reshape(rows_all, width),
        norm_gain.reshape(1, width),
        router.T,
        jnp.swapaxes(choices, 1, 2),
        expert_in.reshape(2 * hidden, width),
        expert_out.reshape(hidden, width),
    )
    return moe.reshape(micro, rows, slice_width)


def solution(mesh):
    return jax.shard_map(
        body,
        mesh=mesh,
        in_specs=(
            P(None, "section", None),
            P(),
            P(),
            P("section", None, "inner", None),
            P("section", "inner", None),
            P(None, "section", None),
        ),
        out_specs=P(None, "section", "inner"),
        check_vma=False,
    )
```
